32 devices in a mesh: dp: 8 (over z, x), tensor: 4 (over y, core).
Axes of the slice: x: 2, y: 2, z: 4, core: 2. Of those that a mesh axis runs over, the one named last changes fastest.
Arguments:
- clips: bfloat16 [16, 16, 196, 768], P('dp', 'tensor'), may hold values from -6 to 6
- cotangent: bfloat16 [16, 16, 196, 768], P('dp', 'tensor'), may hold values from -6 to 6
- ln_gain: float32 [3, 768], replicated, may hold values from 0.5 to 1.5
- ln_shift: float32 [3, 768], replicated, may hold values from -2 to 2
- attn_qkv: bfloat16 [2, 3, 768, 768], P(None, None, None, 'tensor'), may hold values from -0.21875 to 0.21875
- attn_qv_bias: float32 [2, 2, 768], P(None, None, 'tensor'), may hold values from -2 to 2
- attn_out: bfloat16 [2, 768, 768], P(None, 'tensor'), may hold values from -0.875 to 0.875
- attn_out_bias: float32 [2, 768], replicated, may hold values from -2 to 2
- mlp_in: bfloat16 [768, 3072], P(None, 'tensor'), may hold values from -0.21875 to 0.21875
- mlp_in_bias: float32 [3072], P('tensor'), may hold values from -2 to 2
- mlp_out: bfloat16 [3072, 768], P('tensor'), may hold values from -0.109375 to 0.109375
- mlp_out_bias: float32 [768], replicated, may hold values from -2 to 2
Outputs:
- output: float32 [16, 16, 196, 768], P('dp', 'tensor')
- input_grad: float32 [16, 16, 196, 768], P('dp', 'tensor')
- grad_ln_gain: float32 [3, 768], replicated
- grad_ln_shift: float32 [3, 768], replicated
- grad_attn_qkv: float32 [2, 3, 768, 768], P(None, None, None, 'tensor')
- grad_attn_qv_bias: float32 [2, 2, 768], P(None, None, 'tensor')
- grad_attn_out: float32 [2, 768, 768], P(None, 'tensor')
- grad_attn_out_bias: float32 [2, 768], replicated
- grad_mlp_in: float32 [768, 3072], P(None, 'tensor')
- grad_mlp_in_bias: float32 [3072], P('tensor')
- grad_mlp_out: float32 [3072, 768], P('tensor')
- grad_mlp_out_bias: float32 [768], replicated
The draws below stay inside these ranges and needn't reach their ends.
All inputs are finite; a program needn't handle non-finite values.
Results may differ from the reference program's by a relative error of at most 0.025.
Values may be sent and summed in bfloat16 or wider, within the bound.
A program may use at most 256 MiB of HBM per device.

```python
import jax
import jax.numpy as jnp
from jax import lax

D = 768
HEADS = 12
HEAD_DIM = 64
FF = 3072
FRAMES = 16
PLACES = 196
CLIPS = 16


def level_of(stream_key, shape, pieces, smallest, high):
    factor_of = 1.0
    for dim, shards_of in pieces:
        steps = jax.random.uniform(jax.random.fold_in(jax.random.fold_in(stream_key, 6), dim), (shards_of,), jnp.float32, smallest / len(pieces), high / len(pieces))
        factor_of = factor_of * jnp.repeat(jnp.exp(steps), shape[dim] // shards_of).reshape((-1,) + (1,) * (len(shape) - 1 - dim))
    return factor_of


def normal_values(own_key, dims, deviation, bound, shards=(), kind=jnp.bfloat16):
    factor_of = level_of(own_key, dims, shards, -0.22, 0.18) if shards else 1.0
    values = jax.random.normal(own_key, dims, jnp.float32) * deviation * factor_of
    return jnp.minimum(jnp.maximum(values, -bound), bound).astype(kind)


def setup_inputs(seed: int = 0) -> dict:
    key_list = jax.random.split(jax.random.key(seed), 13)
    clips = normal_values(key_list[0], (CLIPS, FRAMES, PLACES, D), 1.0, 6.0, ((0, 8), (1, 4)))
    cotangent = normal_values(key_list[1], (CLIPS, FRAMES, PLACES, D), 1.0, 6.0, ((0, 8), (1, 4)))
    ln_gain = jnp.clip(1.0 + 0.1 * jax.random.normal(key_list[2], (3, D), jnp.float32), 0.5, 1.5)
    ln_shift = normal_values(key_list[3], (3, D), 0.3, 2.0, (), jnp.float32)
    attn_qkv = normal_values(key_list[4], (2, 3, D, D), D ** -0.5, 0.21875, ((3, 4),))
    attn_qv_bias = normal_values(key_list[5], (2, 2, D), 0.3, 2.0, ((2, 4),), jnp.float32)
    attn_out = normal_values(key_list[6], (2, D, D), (D // 16) ** -0.5, 0.875, ((1, 4),))
    attn_out_bias = normal_values(key_list[7], (2, D), 0.3, 2.0, (), jnp.float32)
    mlp_in = normal_values(key_list[8], (D, FF), D ** -0.5, 0.21875, ((1, 4),))
    mlp_in_bias = normal_values(key_list[9], (FF,), 0.3, 2.0, ((0, 4),), jnp.float32)
    mlp_out = normal_values(key_list[10], (FF, D), FF ** -0.5, 0.109375, ((0, 4),))
    mlp_out_bias = normal_values(key_list[11], (D,), 0.3, 2.0, (), jnp.float32)
    return {"clips": clips, "cotangent": cotangent, "ln_gain": ln_gain, "ln_shift": ln_shift, "attn_qkv": attn_qkv, "attn_qv_bias": attn_qv_bias, "attn_out": attn_out, "attn_out_bias": attn_out_bias, "mlp_in": mlp_in, "mlp_in_bias": mlp_in_bias, "mlp_out": mlp_out, "mlp_out_bias": mlp_out_bias}


@jax.custom_vjp
def low(v):
    return lax.optimization_barrier(v.astype(jnp.bfloat16)).astype(jnp.float32)

@jax.custom_vjp
def low_back(v):
    return v

def low_keep(v):
    return (low(v), None)

def low_pass(kept, grad):
    return (grad,)

def back_keep(v):
    return (v, None)

def back_low(kept, grad):
    return (low(grad),)
low.defvjp(low_keep, low_pass)
low_back.defvjp(back_keep, back_low)
norm_epsilon = 1e-06
highest = lax.Precision.HIGHEST

def norm_layer(values, norm_gain, norm_shift):
    row_mean = lax.optimization_barrier(jnp.mean(values, axis=-1, keepdims=True))
    centered = values - row_mean
    variance = lax.optimization_barrier(jnp.mean(centered * centered, axis=-1, keepdims=True))
    return centered * lax.rsqrt(variance + norm_epsilon) * norm_gain + norm_shift

def pair_scores(first_side, second_side, temporal):
    if temporal:
        return jnp.einsum('fphe,gphe->phfg', first_side, second_side, precision=highest)
    return jnp.einsum('fphe,fqhe->fhpq', first_side, second_side, precision=highest)

def weigh_rows(shares, values, temporal):
    if temporal:
        return jnp.einsum('phfg,gphe->fphe', shares, values, precision=highest)
    return jnp.einsum('fhpq,fqhe->fphe', shares, values, precision=highest)

def attend(normed, w_qkv, b_qv, w_out, b_out, temporal):
    frames, places = (normed.shape[0], normed.shape[1])
    projected = jnp.einsum('fpd,cde->cfpe', normed, w_qkv, precision=highest)
    queries = low(low_back(projected[0] + b_qv[0])).reshape(frames, places, HEADS, HEAD_DIM)
    key_vecs = low(low_back(projected[1])).reshape(frames, places, HEADS, HEAD_DIM)
    value_vecs = low(low_back(projected[2] + b_qv[1])).reshape(frames, places, HEADS, HEAD_DIM)
    scores = low_back(pair_scores(queries, key_vecs, temporal) * HEAD_DIM ** (-0.5))
    shares = low(jax.nn.softmax(scores, axis=-1))
    context = low(low_back(weigh_rows(shares, value_vecs, temporal))).reshape(frames, places, D)
    branch = low_back(jnp.einsum('fpe,ed->fpd', context, w_out, precision=highest))
    return branch + b_out

def layer(stream, gains, shifts, w_qkv, b_qv, w_out, b_out, w_in, b_in, w_down, b_down):
    normed = low(norm_layer(stream, gains[0], shifts[0]))
    stream = stream + attend(normed, w_qkv[0], b_qv[0], w_out[0], b_out[0], False)
    normed = low(norm_layer(stream, gains[1], shifts[1]))
    stream = stream + attend(normed, w_qkv[1], b_qv[1], w_out[1], b_out[1], True)
    normed = low(norm_layer(stream, gains[2], shifts[2]))
    raised = low_back(jnp.einsum('fpd,dh->fph', normed, w_in, precision=highest) + b_in)
    hidden = low(jax.nn.gelu(raised, approximate=False))
    branch = low_back(jnp.einsum('fph,hd->fpd', hidden, w_down, precision=highest))
    return stream + (branch + b_down)

def reference(clips, cotangent, ln_gain, ln_shift, attn_qkv, attn_qv_bias, attn_out, attn_out_bias, mlp_in, mlp_in_bias, mlp_out, mlp_out_bias):
    params = (ln_gain, ln_shift, attn_qkv, attn_qv_bias, attn_out, attn_out_bias, mlp_in, mlp_in_bias, mlp_out, mlp_out_bias)
    params = jax.tree.map(lambda weight_arr: weight_arr.astype(jnp.float32), params)
    zero_grads = jax.tree.map(jnp.zeros_like, params)

    def per_clip(accum, clip_pair):
        clip_in, clip_cot = clip_pair
        result, pull_back = jax.vjp(layer, clip_in.astype(jnp.float32), *params)
        grads_all = pull_back(clip_cot.astype(jnp.float32))
        accum = jax.tree.map(jnp.add, accum, tuple(grads_all[1:]))
        return (accum, (result, grads_all[0]))
    accum, (results, input_grads) = lax.scan(per_clip, zero_grads, (clips, cotangent))
    return (results, input_grads, accum[0], accum[1], accum[2], accum[3], accum[4], accum[5], accum[6], accum[7], accum[8], accum[9])
```

```python
import jax
import jax.numpy as jnp
from jax import lax
from jax.sharding import PartitionSpec as P

HEAD_DIM = 64
norm_epsilon = 1e-06
ROWS = 200
HALF = 104
STEP = 96
BF = jnp.bfloat16
F32 = jnp.float32


def dot(spec, a, b):
    return jnp.einsum(spec, a, b, preferred_element_type=F32)


def norm_stats(values):
    mean = jnp.mean(values, axis=-1, keepdims=True)
    centered = values - mean
    inv = lax.rsqrt(jnp.mean(centered * centered, axis=-1, keepdims=True) + norm_epsilon)
    return centered * inv, inv


def norm_back(values, gain, grad):
    hat, inv = norm_stats(values)
    e = grad * gain
    dv = inv * (
        e - jnp.mean(e, axis=-1, keepdims=True) - hat * jnp.mean(e * hat, axis=-1, keepdims=True)
    )
    dims = tuple(range(grad.ndim - 1))
    return dv, jnp.sum(grad * hat, axis=dims), jnp.sum(grad, axis=dims)


def heads(v):
    return v.reshape(v.shape[:-1] + (v.shape[-1] // HEAD_DIM, HEAD_DIM))


def attention(normed, w, mask):
    wq, wk, wv, wo, bq, bv = w
    q = (dot("grd,ed->gre", normed, wq) + bq).astype(BF)
    k = dot("grd,ed->gre", normed, wk).astype(BF)
    v = (dot("grd,ed->gre", normed, wv) + bv).astype(BF)
    s = dot("gqhe,gkhe->ghqk", heads(q), heads(k)) * HEAD_DIM**-0.5
    s = jnp.where(mask, s, -1e30)
    top = jnp.max(s, axis=-1, keepdims=True)
    ex = jnp.exp(s - top)
    total = jnp.sum(ex, axis=-1, keepdims=True)
    p = (ex / total).astype(BF)
    o = dot("ghqk,gkhe->gqhe", p, heads(v)).astype(BF).reshape(normed.shape)
    return q, k, v, o, top + jnp.log(total)


def attention_back(normed, kept, w, mask, grad):
    wq, wk, wv, wo, bq, bv = w
    q, k, v, o, lse = kept
    shape = normed.shape
    do = dot("grd,ed->gre", grad, wo).astype(BF)
    gwo = dot("gre,grd->ed", o, grad)
    s = dot("gqhe,gkhe->ghqk", heads(q), heads(k)) * HEAD_DIM**-0.5
    p = jnp.where(mask, jnp.exp(s - lse), 0.0)
    dp = dot("gqhe,gkhe->ghqk", heads(do), heads(v))
    ds = (p * (dp - jnp.sum(p * dp, axis=-1, keepdims=True))).astype(BF)
    dq = (dot("ghqk,gkhe->gqhe", ds, heads(k)) * HEAD_DIM**-0.5).astype(BF).reshape(shape)
    dk = (dot("ghqk,gqhe->gkhe", ds, heads(q)) * HEAD_DIM**-0.5).astype(BF).reshape(shape)
    dv = dot("ghqk,gqhe->gkhe", p.astype(BF), heads(do)).astype(BF).reshape(shape)
    gq = dot("gre,grd->ed", dq, normed)
    gk = dot("gre,grd->ed", dk, normed)
    gv = dot("gre,grd->ed", dv, normed)
    dn = dot("gre,ed->grd", dq, wq) + dot("gre,ed->grd", dk, wk) + dot("gre,ed->grd", dv, wv)
    bias = (jnp.sum(dq, axis=(0, 1), dtype=F32), jnp.sum(dv, axis=(0, 1), dtype=F32))
    return dn.astype(BF), (gq, gk, gv, gwo), bias


def shards(clips, cot, gain, shift, qkv, qvb, wout, bout, win, b_in, wdown, bdown):
    tensor = lax.axis_index("tensor")
    y, core = tensor // 2, tensor % 2
    x = lax.axis_index("dp") % 2
    dp = lax.axis_size("dp")
    width = clips.shape[-1]
    places = clips.shape[2]

    def over_tensor(v, bit):
        return lax.ppermute(v, "tensor", [(i, i ^ bit) for i in range(4)])

    def over_dp(v, bit):
        return lax.ppermute(v, "dp", [(i, i ^ bit) for i in range(dp)])

    def pad(v):
        return jnp.pad(v, ((0, 0), (0, ROWS - places), (0, 0)))

    def split(a, b):
        return jnp.where(x == 0, a, b), jnp.where(x == 0, b, a)

    def whole_clip(v):
        mine = pad(lax.dynamic_index_in_dim(v, y, 0, False))
        other = pad(lax.dynamic_index_in_dim(v, 1 - y, 0, False))
        return jnp.concatenate([mine, over_tensor(other, 2)])

    def back(v):
        n = v.shape[0] // 2
        v = v[:, :places]
        got = over_tensor(v[n:], 2)
        a, b = v[:n], got
        first = jnp.where(y == 0, a, b)
        second = jnp.where(y == 0, b, a)
        return jnp.stack([first, second]).astype(F32)

    def hi_lo(v):
        hi = v.astype(BF)
        return hi, (v - hi.astype(F32)).astype(BF)

    def gather(halves):
        send, keep = split(*halves)
        gy = over_tensor(send, 2)
        gx = over_dp(gy, 1)
        two = split(gy, gx)
        three = tuple(over_tensor(v, 1) for v in two)
        one = tuple(over_tensor(v, 1) for v in halves)
        return [halves, one, two, three]

    e = qkv.shape[-1]

    def attn_weights(i):
        hi, lo = hi_lo(qvb[i].reshape(1, -1))
        rows = jnp.concatenate([hi, lo], axis=1)
        rows = jnp.concatenate([rows, jnp.zeros((7, width), BF)])
        a = jnp.concatenate([qkv[i, 0].T, qkv[i, 1].T, rows])
        b = jnp.concatenate([qkv[i, 2].T, wout[i], jnp.zeros((8, width), BF)])
        got = gather((a, b))
        wq = jnp.concatenate([g[0][:e] for g in got])
        wk = jnp.concatenate([g[0][e : 2 * e] for g in got])
        wv = jnp.concatenate([g[1][:e] for g in got])
        wo = jnp.concatenate([g[1][e : 2 * e] for g in got])
        bias = [g[0][2 * e].astype(F32) for g in got]
        bias = [v[: 2 * e] + v[2 * e :] for v in bias]
        bq = jnp.concatenate([v[:e] for v in bias])
        bv = jnp.concatenate([v[e:] for v in bias])
        return wq, wk, wv, wo, bq, bv

    def mlp_weights():
        h = win.shape[1] // 2
        wt = win.T
        out = []
        for k in range(2):
            hi, lo = hi_lo(b_in[k * h : (k + 1) * h].reshape(1, -1))
            rows = jnp.concatenate([jnp.concatenate([hi, lo], axis=1), jnp.zeros((7, width), BF)])
            out.append(
                jnp.concatenate([wt[k * h : (k + 1) * h], wdown[k * h : (k + 1) * h], rows])
            )
        got = gather(tuple(out))
        res = []
        for g in got:
            bias = [v[2 * h].astype(F32) for v in g]
            bias = jnp.concatenate([v[:h] + v[h:] for v in bias])
            res.append(
                (
                    jnp.concatenate([v[:h] for v in g]),
                    jnp.concatenate([v[h : 2 * h] for v in g]),
                    bias,
                )
            )
        return res

    def to_places(v):
        own = lax.dynamic_slice_in_dim(v, STEP * core, HALF, 1)
        send = lax.dynamic_slice_in_dim(v, STEP * (1 - core), HALF, 1)
        both = jnp.concatenate([own, over_tensor(send, 1)])
        f = both.shape[0]
        both = both.reshape(f, HALF // 8, 8, width).transpose(1, 0, 2, 3)
        return both.reshape(HALF // 8, f * 8, width)

    def to_frames(v, flip=False):
        f = v.shape[1] // 8
        v = v.reshape(HALF // 8, f, 8, width).transpose(1, 0, 2, 3).reshape(f, HALF, width)
        own = v[: f // 2]
        got = over_tensor(v[f // 2 :], 1)
        if flip:
            got = jnp.concatenate([got[..., i * e : (i + 1) * e] for i in (1, 0, 3, 2)], axis=-1)
        cut = 2 * HALF - ROWS
        a = jnp.concatenate([own, got[:, cut:]], axis=1)
        b = jnp.concatenate([got, own[:, cut:]], axis=1)
        return jnp.where(core == 0, a, b)

    stream0 = whole_clip(clips).astype(F32)
    w0 = attn_weights(0)
    w1 = attn_weights(1)
    wm = mlp_weights()
    grad3b = whole_clip(cot)
    row = lax.broadcasted_iota(jnp.int32, (ROWS, ROWS), 1)
    mask0 = row < places
    frames = 2 * stream0.shape[0]
    r0 = lax.broadcasted_iota(jnp.int32, (frames * 8, frames * 8), 0) % 8
    r1 = lax.broadcasted_iota(jnp.int32, (frames * 8, frames * 8), 1) % 8
    mask1 = r0 == r1

    n0 = (norm_stats(stream0)[0] * gain[0] + shift[0]).astype(BF)
    kept0 = attention(n0, w0, mask0)
    stream1 = stream0 + (dot("gre,ed->grd", kept0[3], w0[3]) + bout[0])
    n1 = (norm_stats(stream1)[0] * gain[1] + shift[1]).astype(BF)
    n1p = to_places(n1)
    kept1 = attention(n1p, w1, mask1)
    o1 = to_frames(kept1[3], True)
    stream2 = stream1 + (dot("gre,ed->grd", o1, w1[3]) + bout[1])
    n2 = (norm_stats(stream2)[0] * gain[2] + shift[2]).astype(BF)

    branch = 0.0
    dn2 = 0.0
    gmlp = [None] * 4
    grad3 = grad3b.astype(F32)
    for r in (3, 1, 2, 0):
        wt, wd, b = wm[r]
        raised = dot("grd,hd->grh", n2, wt) + b
        hidden, pull = jax.vjp(lambda u: jax.nn.gelu(u, approximate=False), raised)
        hidden = hidden.astype(BF)
        branch = branch + dot("grh,hd->grd", hidden, wd)
        dh = dot("grd,hd->grh", grad3b, wd)
        dr = pull(dh)[0].astype(BF)
        gmlp[r] = (
            dot("grh,grd->hd", dr, n2),
            dot("grh,grd->hd", hidden, grad3b),
            jnp.sum(dr, axis=(0, 1), dtype=F32),
        )
        dn2 = dn2 + dot("grh,hd->grd", dr, wt)
    output = back((stream2 + (branch + bdown)).astype(BF))
    gbdown = jnp.sum(grad3, axis=(0, 1))
    dv, gg2, gs2 = norm_back(stream2, gain[2], dn2)
    grad2 = grad3 + dv
    gbo1 = jnp.sum(grad2, axis=(0, 1))
    g2p = to_places(grad2.astype(BF))
    place = STEP * core + 8 * lax.broadcasted_iota(jnp.int32, (HALF // 8, 1, 1), 0)
    g2p = jnp.where((core == 1) & (place < HALF), jnp.zeros_like(g2p), g2p)
    dn1p, gw1, gb1 = attention_back(n1p, kept1, w1, mask1, g2p)
    dv, gg1, gs1 = norm_back(stream1, gain[1], to_frames(dn1p).astype(F32))
    grad1 = grad2 + dv
    gbo0 = jnp.sum(grad1, axis=(0, 1))
    dn0, gw0, gb0 = attention_back(n0, kept0, w0, mask0, grad1.astype(BF))
    dv, gg0, gs0 = norm_back(stream0, gain[0], dn0.astype(F32))
    input_grad = back((grad1 + dv).astype(BF))

    def row_of(v):
        return jnp.zeros((8, width), F32).at[0, : v.shape[0]].set(v)

    def attn_pieces(gw, gb):
        out = []
        for r in range(4):
            s = slice(r * e, (r + 1) * e)
            a = jnp.concatenate([gw[0][s], gw[1][s], row_of(gb[0][s])])
            b = jnp.concatenate([gw[2][s], gw[3][s], row_of(gb[1][s])])
            out.append(split(a.astype(BF), b.astype(BF)))
        return out

    def mlp_pieces():
        h = win.shape[1] // 2
        out = []
        for r in range(4):
            ga, gd, gb = gmlp[r]
            pair = []
            for k in range(2):
                s = slice(k * h, (k + 1) * h)
                pair.append(jnp.concatenate([ga[s], gd[s], row_of(gb[s])]).astype(BF))
            out.append(split(*pair))
        return out

    small = jnp.stack([gg0, gg1, gg2, gs0, gs1, gs2, gbo0, gbo1, gbdown]).astype(BF)
    small = jnp.pad(small, ((0, 7), (0, 0)))

    def reduce_piece(p, extra):
        def both(a, b, swap):
            got = swap(a)
            return b + got

        c1 = over_tensor(jnp.stack([p[1][0], p[3][0]]), 1)
        c2 = over_tensor(jnp.stack([p[1][1], p[3][1]]), 1)
        keep = [p[0][0] + c1[0], p[2][0] + c1[1]]
        send = [p[0][1] + c2[0], p[2][1] + c2[1]]
        got = over_dp(jnp.stack(send), 1)
        keep = [keep[0] + got[0], keep[1] + got[1]]
        total = keep[0] + over_tensor(keep[1], 2)
        if extra is not None:
            extra = extra + over_tensor(extra, 1)
            extra = extra + over_dp(extra, 1)
            extra = extra + over_tensor(extra, 2)
            rows = extra.shape[0]
            total = jnp.concatenate([total, extra])
        bit = 2
        while bit < dp:
            total = total + over_dp(total, bit)
            bit *= 2
        if extra is not None:
            total, extra = total[:-rows], total[-rows:]
        return split(total, over_dp(total, 1)), extra

    (ma, mb), _ = reduce_piece(mlp_pieces(), None)
    (a1, b1), _ = reduce_piece(attn_pieces(gw1, gb1), None)
    (a0, b0), small = reduce_piece(attn_pieces(gw0, gb0), small)
    small = small.astype(F32)

    gqkv = jnp.stack(
        [jnp.stack([a[:e].T, a[e : 2 * e].T, b[:e].T]) for a, b in ((a0, b0), (a1, b1))]
    ).astype(F32)
    gout = jnp.stack([b0[e : 2 * e], b1[e : 2 * e]]).astype(F32)
    gqv = jnp.stack(
        [jnp.stack([a[2 * e, :e], b[2 * e, :e]]) for a, b in ((a0, b0), (a1, b1))]
    ).astype(F32)
    h = win.shape[1] // 2
    gwin = jnp.concatenate([ma[:h], mb[:h]]).T.astype(F32)
    gwd = jnp.concatenate([ma[h : 2 * h], mb[h : 2 * h]]).astype(F32)
    gbin = jnp.concatenate([ma[2 * h, :h], mb[2 * h, :h]]).astype(F32)
    return (
        output,
        input_grad,
        small[0:3],
        small[3:6],
        gqkv,
        gqv,
        gout,
        small[6:8],
        gwin,
        gbin,
        gwd,
        small[8],
    )


def solution(mesh):
    placed = (
        P("dp", "tensor", None, None),
        P("dp", "tensor", None, None),
        P(),
        P(),
        P(None, None, None, "tensor"),
        P(None, None, "tensor"),
        P(None, "tensor", None),
        P(),
        P(None, "tensor"),
        P("tensor"),
        P("tensor", None),
        P(),
    )
    return jax.shard_map(
        shards,
        mesh=mesh,
        in_specs=placed,
        out_specs=(
            P("dp", "tensor", None, None),
            P("dp", "tensor", None, None),
            P(),
            P(),
            P(None, None, None, "tensor"),
            P(None, None, "tensor"),
            P(None, "tensor", None),
            P(),
            P(None, "tensor"),
            P("tensor"),
            P("tensor", None),
            P(),
        ),
        check_vma=False,
    )
```

```python
import functools

import jax
import jax.numpy as jnp
from jax import lax
from jax.experimental import pallas as pl
from jax.experimental.pallas import tpu as pltpu
from jax.sharding import PartitionSpec as P

BF = jnp.bfloat16
F32 = jnp.float32
HEAD_DIM = 64
norm_epsilon = 1e-06
LIMIT = 60 << 20


def nn(a, b):
    return lax.dot_general(a, b, (((1,), (0,)), ((), ())), preferred_element_type=F32)


def nt(a, b):
    return lax.dot_general(a, b, (((1,), (1,)), ((), ())), preferred_element_type=F32)


def tn(a, b):
    return lax.dot_general(a, b, (((0,), (0,)), ((), ())), preferred_element_type=F32)


def hat_of(values):
    mean = jnp.mean(values, axis=-1, keepdims=True)
    centered = values - mean
    inv = lax.rsqrt(jnp.mean(centered * centered, axis=-1, keepdims=True) + norm_epsilon)
    return centered * inv, inv


def hat_back(hat, inv, gain, grad):
    e = grad * gain
    return inv * (
        e - jnp.mean(e, axis=-1, keepdims=True) - hat * jnp.mean(e * hat, axis=-1, keepdims=True)
    )


GROUP = 256
PER = GROUP // HEAD_DIM


def head_of_lane(rows):
    return lax.broadcasted_iota(jnp.int32, (rows, GROUP), 1) // HEAD_DIM


def stacked(v):
    lane = head_of_lane(v.shape[0])
    return jnp.concatenate([jnp.where(lane == h, v, jnp.zeros_like(v)) for h in range(PER)])


def unstacked(v):
    rows = v.shape[0] // PER
    lane = head_of_lane(rows)
    out = v[:rows]
    for h in range(1, PER):
        out = jnp.where(lane == h, v[h * rows : (h + 1) * rows], out)
    return out


def only_places(places):
    def mask(s):
        cut = places // 8 * 8
        row = lax.broadcasted_iota(jnp.int32, (s.shape[0] - cut, s.shape[1]), 0)
        return jnp.concatenate([s[:cut], jnp.where(row < places - cut, s[cut:], -1e30)])

    return mask


def same_place(bias):
    return lambda s: s + bias


def place_bias(rows):
    a = lax.broadcasted_iota(jnp.int32, (rows, PER * rows), 0) & 7
    b = lax.broadcasted_iota(jnp.int32, (rows, PER * rows), 1) & 7
    return jnp.where(a == b, 0.0, -1e30).astype(F32)


def attend(q_ref, k_ref, v_ref, o_ref, lse_ref, mask):
    for g in range(o_ref.shape[1] // GROUP):
        at = slice(GROUP * g, GROUP * g + GROUP)
        s = mask(nt(k_ref[:, at], stacked(q_ref[:, at])))
        top = jnp.max(s, axis=0, keepdims=True)
        ex = jnp.exp(s - top)
        total = jnp.sum(ex, axis=0, keepdims=True)
        p = (ex * (1.0 / total)).astype(BF)
        o_ref[:, at] = unstacked(tn(p, v_ref[:, at])).astype(BF)
        lse_ref[g : g + 1] = top + jnp.log(total)


def attend_back(q_ref, k_ref, v_ref, do_ref, lse_ref, dq_ref, dk_ref, dv_ref, mask):
    for g in range(do_ref.shape[1] // GROUP):
        at = slice(GROUP * g, GROUP * g + GROUP)
        qs, dos = stacked(q_ref[:, at]), stacked(do_ref[:, at])
        k = k_ref[:, at]
        p = jnp.exp(mask(nt(k, qs)) - lse_ref[g : g + 1])
        dp = nt(v_ref[:, at], dos)
        ds = (p * (dp - jnp.sum(p * dp, axis=0, keepdims=True))).astype(BF)
        dv_ref[:, at] = nn(p.astype(BF), dos).astype(BF)
        dk_ref[:, at] = nn(ds, qs).astype(BF)
        dq_ref[:, at] = (unstacked(tn(ds, k)) * HEAD_DIM**-0.5).astype(BF)


def whole(shape):
    return pl.BlockSpec(shape, lambda *_: (0,) * len(shape), pipeline_mode=pl.Buffered(1))


def params(n=1):
    return pltpu.CompilerParams(
        dimension_semantics=("arbitrary",) * n, vmem_limit_bytes=LIMIT
    )


def spatial_body(places, x, w, wo, vec, stream, n1, q, k, v, o, lse):
    xv = x[0].astype(F32)
    d = xv.shape[1]
    n0 = (hat_of(xv)[0] * vec[0:1] + vec[1:2]).astype(BF)
    q[0] = ((nt(n0, w[0:d]) + vec[2:3]) * HEAD_DIM**-0.5).astype(BF)
    k[0] = nt(n0, w[d : 2 * d]).astype(BF)
    v[0] = (nt(n0, w[2 * d : 3 * d]) + vec[3:4]).astype(BF)
    attend(q.at[0], k.at[0], v.at[0], o.at[0], lse.at[0], only_places(places))
    s1 = xv + (nn(o[0], wo[...]) + vec[4:5])
    stream[0] = s1
    n1[0] = (hat_of(s1)[0] * vec[5:6] + vec[6:7]).astype(BF)


def spatial(x, w, wo, vec, places):
    f, r, d = x.shape
    blk = pl.BlockSpec((1, r, d), lambda i: (i, 0, 0))
    big = jax.ShapeDtypeStruct((f, r, d), BF)
    return pl.pallas_call(
        functools.partial(spatial_body, places),
        grid=(f,),
        in_specs=[blk, whole(w.shape), whole(wo.shape), whole(vec.shape)],
        out_specs=[blk] * 6 + [pl.BlockSpec((1, d // GROUP, PER * r), lambda i: (i, 0, 0))],
        out_shape=[jax.ShapeDtypeStruct((f, r, d), F32)]
        + [big] * 5
        + [jax.ShapeDtypeStruct((f, d // GROUP, PER * r), F32)],
        compiler_params=params(),
        name="spatial",
    )(x, w, wo, vec)


def temporal_body(n1, w, vec, q, k, v, o, lse):
    n = n1[0]
    d = n.shape[1]
    q[0] = ((nt(n, w[0:d]) + vec[0:1]) * HEAD_DIM**-0.5).astype(BF)
    k[0] = nt(n, w[d : 2 * d]).astype(BF)
    v[0] = (nt(n, w[2 * d : 3 * d]) + vec[1:2]).astype(BF)
    attend(q.at[0], k.at[0], v.at[0], o.at[0], lse.at[0], same_place(place_bias(n.shape[0])))


def temporal(n1, w, vec):
    b, r, d = n1.shape
    blk = pl.BlockSpec((1, r, d), lambda i: (i, 0, 0))
    return pl.pallas_call(
        temporal_body,
        grid=(b,),
        in_specs=[blk, whole(w.shape), whole(vec.shape)],
        out_specs=[blk] * 4 + [pl.BlockSpec((1, d // GROUP, PER * r), lambda i: (i, 0, 0))],
        out_shape=[jax.ShapeDtypeStruct((b, r, d), BF)] * 4
        + [jax.ShapeDtypeStruct((b, d // GROUP, PER * r), F32)],
        compiler_params=params(),
        name="temporal",
    )(n1, w, vec)


def temporal_back_body(g, n, q, k, v, o, lse, w, wo, dn, gw, gwo, sums, dqkv, do):
    i = pl.program_id(0)
    d = g.shape[-1]
    r = q.shape[1]
    do[...] = nt(g[pl.ds(i, 1)][0], wo[...]).astype(BF)
    attend_back(
        q.at[0], k.at[0], v.at[0], do, lse.at[0],
        dqkv.at[0, i], dqkv.at[1, i], dqkv.at[2, i], same_place(place_bias(r)),
    )

    @pl.when(i == pl.num_programs(0) - 1)
    def _():
        rows = g.shape[0] * r
        nv = n[...].reshape(rows, d)
        for c in range(3):
            dv = dqkv[c].reshape(rows, d)
            gw[c * d : (c + 1) * d] = tn(dv, nv).astype(BF)
            sums[c : c + 1] = jnp.sum(dv.astype(F32), axis=0, keepdims=True)
        gwo[...] = tn(o[...].reshape(rows, d), g[...].reshape(rows, d)).astype(BF)
        acc = nn(dqkv[0].reshape(rows, d), w[0:d])
        acc += nn(dqkv[1].reshape(rows, d), w[d : 2 * d])
        acc += nn(dqkv[2].reshape(rows, d), w[2 * d : 3 * d])
        dn[...] = acc.astype(BF).reshape(dn.shape)


def temporal_back(g, n, q, k, v, o, lse, w, wo):
    b, r, d = g.shape
    blk = pl.BlockSpec((1, r, d), lambda i: (i, 0, 0))
    return pl.pallas_call(
        temporal_back_body,
        grid=(b,),
        in_specs=[whole(g.shape), whole(n.shape), blk, blk, blk, whole(o.shape),
                  pl.BlockSpec((1, d // GROUP, PER * r), lambda i: (i, 0, 0)), whole(w.shape), whole(wo.shape)],
        out_specs=[whole(g.shape), whole(w.shape), whole(wo.shape), whole((8, d))],
        out_shape=[jax.ShapeDtypeStruct(g.shape, BF), jax.ShapeDtypeStruct(w.shape, BF),
                   jax.ShapeDtypeStruct(wo.shape, BF), jax.ShapeDtypeStruct((8, d), F32)],
        scratch_shapes=[pltpu.VMEM((3, b, r, d), BF), pltpu.VMEM((r, d), BF)],
        compiler_params=params(),
        name="temporal_back",
    )(g, n, q, k, v, o, lse, w, wo)


def spatial_back_body(places, x, s1, dn1, g2, q, k, v, o, lse, w, wo, vec,
                      g0, gw, gwo, sums, dqkv, n0s, gbs, os, do):
    i = pl.program_id(0)
    r, d = x.shape[1:]

    @pl.when(i == 0)
    def _():
        sums[...] = jnp.zeros_like(sums)

    def add(at, val):
        sums[at : at + 1] += jnp.sum(val, axis=0, keepdims=True)

    hat, inv = hat_of(s1[0])
    dn = dn1[0].astype(F32)
    add(2, dn * hat)
    add(3, dn)
    g1 = g2[0] + hat_back(hat, inv, vec[2:3], dn)
    add(4, g1)
    gb = g1.astype(BF)
    gbs[i] = gb
    os[i] = o[0]
    do[...] = nt(gb, wo[...]).astype(BF)
    attend_back(
        q.at[0], k.at[0], v.at[0], do, lse.at[0],
        dqkv.at[0, i], dqkv.at[1, i], dqkv.at[2, i], only_places(places),
    )
    hat, inv = hat_of(x[0].astype(F32))
    n0s[i] = (hat * vec[0:1] + vec[1:2]).astype(BF)
    dn = nn(dqkv[0, i], w[0:d]) + nn(dqkv[1, i], w[d : 2 * d]) + nn(dqkv[2, i], w[2 * d : 3 * d])
    add(0, dn * hat)
    add(1, dn)
    g0[0] = g1 + hat_back(hat, inv, vec[0:1], dn)

    @pl.when(i == pl.num_programs(0) - 1)
    def _():
        rows = n0s.shape[0] * r
        nv = n0s[...].reshape(rows, d)
        for c in range(3):
            dv = dqkv[c].reshape(rows, d)
            gw[c * d : (c + 1) * d] = tn(dv, nv).astype(BF)
            sums[5 + c : 6 + c] = jnp.sum(dv.astype(F32), axis=0, keepdims=True)
        gwo[...] = tn(os[...].reshape(rows, d), gbs[...].reshape(rows, d)).astype(BF)


def spatial_back(x, s1, dn1, g2, q, k, v, o, lse, w, wo, vec, places):
    f, r, d = x.shape
    blk = pl.BlockSpec((1, r, d), lambda i: (i, 0, 0))
    return pl.pallas_call(
        functools.partial(spatial_back_body, places),
        grid=(f,),
        in_specs=[blk] * 8 + [pl.BlockSpec((1, d // GROUP, PER * r), lambda i: (i, 0, 0)),
                  whole(w.shape), whole(wo.shape), whole(vec.shape)],
        out_specs=[blk, whole(w.shape), whole(wo.shape), whole((8, d))],
        out_shape=[jax.ShapeDtypeStruct(x.shape, F32), jax.ShapeDtypeStruct(w.shape, BF),
                   jax.ShapeDtypeStruct(wo.shape, BF), jax.ShapeDtypeStruct((8, d), F32)],
        scratch_shapes=[pltpu.VMEM((3, f, r, d), BF)] + [pltpu.VMEM((f, r, d), BF)] * 3
        + [pltpu.VMEM((r, d), BF)],
        compiler_params=params(),
        name="spatial_back",
    )(x, s1, dn1, g2, q, k, v, o, lse, w, wo, vec)


def gelu_parts(u):
    cdf = 0.5 + 0.5 * lax.erf(u * 0.7071067811865476)
    return u * cdf, cdf + u * (jnp.exp(-0.5 * u * u) * 0.3989422804014327)


def mlp_step(n2, gb, wt, wd, b, s, branch, dn, gwt, gwd, gbi):
    u = nt(n2, wt[s]) + b[s]
    h, slope = gelu_parts(u)
    h = h.astype(BF)
    branch[...] += nn(h, wd[s])
    dr = (nt(gb, wd[s]) * slope).astype(BF)
    dn[...] += nn(dr, wt[s])
    gwt[s] += tn(dr, n2)
    gwd[s] += tn(h, gb)
    gbi[s] += jnp.sum(dr.astype(F32), axis=0, keepdims=True)


def mlp_ends(i, s, gwt, gwd, gbi, gwt_o, gwd_o):
    @pl.when(i == pl.num_programs(0) - 1)
    def _():
        gwt_o[s] = gwt[s].astype(BF)
        gwd_o[s] = gwd[s].astype(BF)


def mlp_first_body(s1, o1, gb, wo, vec, wt, wd, b, s2, n2, branch, dn, gwt_o, gwd_o, gbi, gwt, gwd):
    i, s = pl.program_id(0), pl.program_id(1)

    @pl.when((i == 0) & (s == 0))
    def _():
        gwt[...] = jnp.zeros_like(gwt)
        gwd[...] = jnp.zeros_like(gwd)
        gbi[...] = jnp.zeros_like(gbi)

    @pl.when(s == 0)
    def _():
        v = s1[...] + (nn(o1[...], wo[...]) + vec[0:1])
        s2[...] = v
        n2[...] = (hat_of(v)[0] * vec[1:2] + vec[2:3]).astype(BF)
        branch[...] = jnp.zeros_like(branch)
        dn[...] = jnp.zeros_like(dn)

    mlp_step(n2[...], gb[...], wt, wd, b, s, branch, dn, gwt, gwd, gbi)
    mlp_ends(i, s, gwt, gwd, gbi, gwt_o, gwd_o)


def mlp_first(s1, o1, gb, wo, vec, wt, wd, b, tile):
    rows, d = s1.shape
    ns, h, _ = wt.shape
    blk = pl.BlockSpec((tile, d), lambda i, s: (i, 0))
    sh = lambda t: jax.ShapeDtypeStruct((rows, d), t)
    return pl.pallas_call(
        mlp_first_body,
        grid=(rows // tile, ns),
        in_specs=[blk, blk, blk, whole(wo.shape), whole(vec.shape), whole(wt.shape),
                  whole(wd.shape), whole(b.shape)],
        out_specs=[blk] * 4 + [whole(wt.shape), whole(wd.shape), whole(b.shape)],
        out_shape=[sh(F32), sh(BF), sh(F32), sh(F32), jax.ShapeDtypeStruct(wt.shape, BF),
                   jax.ShapeDtypeStruct(wd.shape, BF), jax.ShapeDtypeStruct(b.shape, F32)],
        scratch_shapes=[pltpu.VMEM(wt.shape, F32), pltpu.VMEM(wd.shape, F32)],
        compiler_params=params(2),
        name="mlp_first",
    )(s1, o1, gb, wo, vec, wt, wd, b)


def mlp_second_body(s2, n2, gb, br0, dn0, vec, wt, wd, b,
                    out, g2, g2b, gwt_o, gwd_o, gbi, sums, branch, dn, gwt, gwd):
    i, s = pl.program_id(0), pl.program_id(1)

    @pl.when((i == 0) & (s == 0))
    def _():
        gwt[...] = jnp.zeros_like(gwt)
        gwd[...] = jnp.zeros_like(gwd)
        gbi[...] = jnp.zeros_like(gbi)
        sums[...] = jnp.zeros_like(sums)

    @pl.when(s == 0)
    def _():
        branch[...] = br0[...]
        dn[...] = dn0[...]

    mlp_step(n2[...], gb[...], wt, wd, b, s, branch, dn, gwt, gwd, gbi)
    mlp_ends(i, s, gwt, gwd, gbi, gwt_o, gwd_o)

    @pl.when(s == pl.num_programs(1) - 1)
    def _():
        def add(at, val):
            sums[at : at + 1] += jnp.sum(val, axis=0, keepdims=True)

        v = s2[...]
        out[...] = (v + (branch[...] + vec[0:1])).astype(out.dtype)
        hat, inv = hat_of(v)
        dv = dn[...]
        add(0, dv * hat)
        add(1, dv)
        g3 = gb[...].astype(F32)
        add(3, g3)
        g = g3 + hat_back(hat, inv, vec[1:2], dv)
        add(2, g)
        g2[...] = g
        g2b[...] = g.astype(BF)


def mlp_second(s2, n2, gb, br0, dn0, vec, wt, wd, b, tile):
    rows, d = s2.shape
    ns, h, _ = wt.shape
    blk = pl.BlockSpec((tile, d), lambda i, s: (i, 0))
    sh = lambda t: jax.ShapeDtypeStruct((rows, d), t)
    return pl.pallas_call(
        mlp_second_body,
        grid=(rows // tile, ns),
        in_specs=[blk] * 5 + [whole(vec.shape), whole(wt.shape), whole(wd.shape), whole(b.shape)],
        out_specs=[blk] * 3 + [whole(wt.shape), whole(wd.shape), whole(b.shape), whole((8, d))],
        out_shape=[sh(F32), sh(F32), sh(BF), jax.ShapeDtypeStruct(wt.shape, BF),
                   jax.ShapeDtypeStruct(wd.shape, BF), jax.ShapeDtypeStruct(b.shape, F32),
                   jax.ShapeDtypeStruct((8, d), F32)],
        scratch_shapes=[pltpu.VMEM((tile, d), F32), pltpu.VMEM((tile, d), F32),
                        pltpu.VMEM(wt.shape, F32), pltpu.VMEM(wd.shape, F32)],
        compiler_params=params(2),
        name="mlp_second",
    )(s2, n2, gb, br0, dn0, vec, wt, wd, b)


ROWS = 208
HALF = ROWS // 2
TILE = 416


def shards(clips, cot, gain, shift, qkv, qvb, wout, bout, win, b_in, wdown, bdown):
    tensor = lax.axis_index("tensor")
    y, core = tensor // 2, tensor % 2
    x = lax.axis_index("dp") % 2
    dp = lax.axis_size("dp")
    width = clips.shape[-1]
    places = clips.shape[2]
    e = qkv.shape[-1]
    h = win.shape[1] // 2

    def over_tensor(v, bit):
        return lax.ppermute(v, "tensor", [(i, i ^ bit) for i in range(4)])

    def over_dp(v, bit):
        return lax.ppermute(v, "dp", [(i, i ^ bit) for i in range(dp)])

    def pad(v):
        return jnp.pad(v, ((0, 0), (0, ROWS - places), (0, 0)))

    def split(a, b):
        return jnp.where(x == 0, a, b), jnp.where(x == 0, b, a)

    def whole_clip(v):
        mine = lax.dynamic_index_in_dim(v, y, 0, False)
        other = lax.dynamic_index_in_dim(v, 1 - y, 0, False)
        return pad(jnp.concatenate([mine, over_tensor(other, 2)]))

    def back(v):
        n = v.shape[0] // 2
        v = v[:, :places]
        got = over_tensor(v[n:].astype(BF), 2).astype(F32)
        mine = v[:n]
        return jnp.stack([jnp.where(y == 0, mine, got), jnp.where(y == 0, got, mine)])

    def hi_lo(v):
        hi = v.astype(BF)
        return hi, (v - hi.astype(F32)).astype(BF)

    def gather(halves):
        send, keep = split(*halves)
        gy = over_tensor(send, 2)
        gx = over_dp(gy, 1)
        two = split(gy, gx)
        three = tuple(over_tensor(v, 1) for v in two)
        one = tuple(over_tensor(v, 1) for v in halves)
        return [halves, one, two, three]

    def attn_weights(i):
        hi, lo = hi_lo(qvb[i].reshape(1, -1))
        rows = jnp.concatenate([hi, lo], axis=1)
        rows = jnp.concatenate([rows, jnp.zeros((7, width), BF)])
        a = jnp.concatenate([qkv[i, 0].T, qkv[i, 1].T, rows])
        b = jnp.concatenate([qkv[i, 2].T, wout[i], jnp.zeros((8, width), BF)])
        got = gather((a, b))
        w = jnp.concatenate(
            [g[0][:e] for g in got] + [g[0][e : 2 * e] for g in got] + [g[1][:e] for g in got]
        )
        wo = jnp.concatenate([g[1][e : 2 * e] for g in got])
        bias = [g[0][2 * e].astype(F32) for g in got]
        bias = [v[: 2 * e] + v[2 * e :] for v in bias]
        return w, wo, jnp.concatenate([v[:e] for v in bias]), jnp.concatenate([v[e:] for v in bias])

    def mlp_weights():
        wt = win.T
        out = []
        for k in range(2):
            hi, lo = hi_lo(b_in[k * h : (k + 1) * h].reshape(1, -1))
            rows = jnp.concatenate([jnp.concatenate([hi, lo], axis=1), jnp.zeros((7, width), BF)])
            out.append(
                jnp.concatenate([wt[k * h : (k + 1) * h], wdown[k * h : (k + 1) * h], rows])
            )
        got = gather(tuple(out))

        def pair(rs):
            a = jnp.stack([jnp.concatenate([v[:h] for v in got[r]]) for r in rs])
            b = jnp.stack([jnp.concatenate([v[h : 2 * h] for v in got[r]]) for r in rs])
            rows = [[v[2 * h].astype(F32) for v in got[r]] for r in rs]
            bias = jnp.stack([jnp.concatenate([v[:h] + v[h:] for v in q]) for q in rows])
            return a, b, bias[:, None, :]

        return pair((3, 1)), pair((2, 0))

    def to_places(v):
        own = lax.dynamic_slice_in_dim(v, HALF * core, HALF, 1)
        send = lax.dynamic_slice_in_dim(v, HALF * (1 - core), HALF, 1)
        both = jnp.concatenate([own, over_tensor(send, 1)])
        f = both.shape[0]
        both = both.reshape(f, HALF // 8, 8, width).transpose(1, 0, 2, 3)
        return both.reshape(HALF // 8, f * 8, width)

    def to_frames(v, flip=False):
        f = v.shape[1] // 8
        v = v.reshape(HALF // 8, f, 8, width).transpose(1, 0, 2, 3).reshape(f, HALF, width)
        own = v[: f // 2]
        got = over_tensor(v[f // 2 :], 1)
        if flip:
            got = jnp.concatenate([got[..., i * e : (i + 1) * e] for i in (1, 0, 3, 2)], axis=-1)
        return jnp.concatenate(
            [jnp.where(core == 0, own, got), jnp.where(core == 0, got, own)], axis=1
        )

    def rows8(*vs):
        return jnp.pad(jnp.stack(vs), ((0, 8 - len(vs)), (0, 0)))

    x0 = whole_clip(clips)
    frames = x0.shape[0]
    flat = (frames * ROWS, width)
    w0, wo0, bq0, bv0 = attn_weights(0)
    w1, wo1, bq1, bv1 = attn_weights(1)
    ma, mb = mlp_weights()
    gb3 = whole_clip(cot).reshape(flat)

    vec = rows8(gain[0], shift[0], bq0, bv0, bout[0], gain[1], shift[1])
    s1, n1, q0, k0, v0, o0, lse0 = spatial(x0, w0, wo0, vec, places)
    n1p = to_places(n1)
    q1, k1, v1, o1p, lse1 = temporal(n1p, w1, rows8(bq1, bv1))
    o1 = to_frames(o1p, True)

    vec = rows8(bout[1], gain[2], shift[2])
    s2, n2, branch, dn2, gwt_a, gwd_a, gb_a = mlp_first(
        s1.reshape(flat), o1.reshape(flat), gb3, wo1, vec, *ma, TILE
    )
    out, g2, g2b, gwt_b, gwd_b, gb_b, sums2 = mlp_second(
        s2, n2, gb3, branch, dn2, rows8(bdown, gain[2]), *mb, TILE
    )
    output = back(out.reshape(x0.shape))

    dn1p, gw1, gwo1, sums1 = temporal_back(
        to_places(g2b.reshape(x0.shape)), n1p, q1, k1, v1, o1p, lse1, w1, wo1
    )
    dn1 = to_frames(dn1p)
    g0, gw0, gwo0, sums0 = spatial_back(
        x0, s1, dn1, g2.reshape(x0.shape), q0, k0, v0, o0, lse0, w0, wo0,
        rows8(gain[0], shift[0], gain[1]), places,
    )
    input_grad = back(g0)

    def row_of(v):
        return jnp.pad(v.astype(BF)[None], ((0, 7), (0, width - v.shape[0])))

    def attn_pieces(gw, gwo, bq, bv):
        out = []
        for r in range(4):
            s = slice(r * e, (r + 1) * e)
            a = jnp.concatenate([gw[:width][s], gw[width : 2 * width][s], row_of(bq[s])])
            b = jnp.concatenate([gw[2 * width :][s], gwo[s], row_of(bv[s])])
            out.append(split(a, b))
        return out

    def mlp_pieces():
        out = []
        for r in range(4):
            at = {3: 0, 1: 1, 2: 0, 0: 1}[r]
            ga, gd, gb = (gwt_a, gwd_a, gb_a) if r in (3, 1) else (gwt_b, gwd_b, gb_b)
            pair = []
            for k in range(2):
                s = slice(k * h, (k + 1) * h)
                pair.append(jnp.concatenate([ga[at, s], gd[at, s], row_of(gb[at, 0, s])]))
            out.append(split(*pair))
        return out

    small = jnp.stack(
        [sums0[0], sums0[2], sums2[0], sums0[1], sums0[3], sums2[1], sums0[4], sums2[2], sums2[3]]
    ).astype(BF)
    small = jnp.pad(small, ((0, 7), (0, 0)))

    def reduce_piece(p, extra):
        c1 = over_tensor(jnp.stack([p[1][0], p[3][0]]), 1)
        c2 = over_tensor(jnp.stack([p[1][1], p[3][1]]), 1)
        keep = [p[0][0] + c1[0], p[2][0] + c1[1]]
        send = [p[0][1] + c2[0], p[2][1] + c2[1]]
        got = over_dp(jnp.stack(send), 1)
        keep = [keep[0] + got[0], keep[1] + got[1]]
        total = keep[0] + over_tensor(keep[1], 2)
        rows = 0
        if extra is not None:
            extra = extra + over_tensor(extra, 1)
            extra = extra + over_dp(extra, 1)
            extra = extra + over_tensor(extra, 2)
            rows = extra.shape[0]
            total = jnp.concatenate([total, extra])
        bit = 2
        while bit < dp:
            total = total + over_dp(total, bit)
            bit *= 2
        if extra is not None:
            total, extra = total[:-rows], total[-rows:]
        return split(total, over_dp(total, 1)), extra

    (ma, mb), _ = reduce_piece(mlp_pieces(), None)
    (a1, b1), _ = reduce_piece(attn_pieces(gw1, gwo1, sums1[0], sums1[2]), None)
    (a0, b0), small = reduce_piece(attn_pieces(gw0, gwo0, sums0[5], sums0[7]), small)
    small = small.astype(F32)

    gqkv = jnp.stack(
        [jnp.stack([a[:e].T, a[e : 2 * e].T, b[:e].T]) for a, b in ((a0, b0), (a1, b1))]
    ).astype(F32)
    gout = jnp.stack([b0[e : 2 * e], b1[e : 2 * e]]).astype(F32)
    gqv = jnp.stack(
        [jnp.stack([a[2 * e, :e], b[2 * e, :e]]) for a, b in ((a0, b0), (a1, b1))]
    ).astype(F32)
    gwin = jnp.concatenate([ma[:h], mb[:h]]).T.astype(F32)
    gwd = jnp.concatenate([ma[h : 2 * h], mb[h : 2 * h]]).astype(F32)
    gbin = jnp.concatenate([ma[2 * h, :h], mb[2 * h, :h]]).astype(F32)
    return (
        output,
        input_grad,
        small[0:3],
        small[3:6],
        gqkv,
        gqv,
        gout,
        small[6:8],
        gwin,
        gbin,
        gwd,
        small[8],
    )


def solution(mesh):
    placed = (
        P("dp", "tensor", None, None),
        P("dp", "tensor", None, None),
        P(),
        P(),
        P(None, None, None, "tensor"),
        P(None, None, "tensor"),
        P(None, "tensor", None),
        P(),
        P(None, "tensor"),
        P("tensor"),
        P("tensor", None),
        P(),
    )
    return jax.shard_map(
        shards,
        mesh=mesh,
        in_specs=placed,
        out_specs=(
            P("dp", "tensor", None, None),
            P("dp", "tensor", None, None),
            P(),
            P(),
            P(None, None, None, "tensor"),
            P(None, None, "tensor"),
            P(None, "tensor", None),
            P(),
            P(None, "tensor"),
            P("tensor"),
            P("tensor", None),
            P(),
        ),
        check_vma=False,
    )
```

```python
import functools

import jax
import jax.numpy as jnp
from jax import lax
from jax.experimental import pallas as pl
from jax.experimental.pallas import tpu as pltpu
from jax.sharding import PartitionSpec as P

BF = jnp.bfloat16
F32 = jnp.float32
HEAD_DIM = 64
norm_epsilon = 1e-06
LIMIT = 60 << 20


def nn(a, b):
    return lax.dot_general(a, b, (((1,), (0,)), ((), ())), preferred_element_type=F32)


def nt(a, b):
    return lax.dot_general(a, b, (((1,), (1,)), ((), ())), preferred_element_type=F32)


def tn(a, b):
    return lax.dot_general(a, b, (((0,), (0,)), ((), ())), preferred_element_type=F32)


def hat_of(values):
    mean = jnp.mean(values, axis=-1, keepdims=True)
    centered = values - mean
    inv = lax.rsqrt(jnp.mean(centered * centered, axis=-1, keepdims=True) + norm_epsilon)
    return centered * inv, inv


def hat_back(hat, inv, gain, grad):
    e = grad * gain
    return inv * (
        e - jnp.mean(e, axis=-1, keepdims=True) - hat * jnp.mean(e * hat, axis=-1, keepdims=True)
    )


GROUP = 256
PER = GROUP // HEAD_DIM


def head_of_lane(rows):
    return lax.broadcasted_iota(jnp.int32, (rows, GROUP), 1) // HEAD_DIM


def stacked(v):
    lane = head_of_lane(v.shape[0])
    return jnp.concatenate([jnp.where(lane == h, v, jnp.zeros_like(v)) for h in range(PER)])


def unstacked(v):
    rows = v.shape[0] // PER
    lane = head_of_lane(rows)
    out = v[:rows]
    for h in range(1, PER):
        out = jnp.where(lane == h, v[h * rows : (h + 1) * rows], out)
    return out


def only_places(places):
    def mask(s):
        cut = places // 8 * 8
        row = lax.broadcasted_iota(jnp.int32, (s.shape[0] - cut, s.shape[1]), 0)
        return jnp.concatenate([s[:cut], jnp.where(row < places - cut, s[cut:], -1e30)])

    return mask


def same_place(bias):
    return lambda s: s + bias


def place_bias(rows):
    a = lax.broadcasted_iota(jnp.int32, (rows, PER * rows), 0) & 7
    b = lax.broadcasted_iota(jnp.int32, (rows, PER * rows), 1) & 7
    return jnp.where(a == b, 0.0, -1e30).astype(F32)


def attend(q_ref, k_ref, v_ref, o_ref, lse_ref, mask):
    for g in range(o_ref.shape[1] // GROUP):
        at = slice(GROUP * g, GROUP * g + GROUP)
        s = mask(nt(k_ref[:, at], stacked(q_ref[:, at])))
        top = jnp.max(s, axis=0, keepdims=True)
        ex = jnp.exp(s - top)
        total = jnp.sum(ex, axis=0, keepdims=True)
        p = (ex * (1.0 / total)).astype(BF)
        o_ref[:, at] = unstacked(tn(p, v_ref[:, at])).astype(BF)
        lse_ref[g : g + 1] = top + jnp.log(total)


def attend_back(q_ref, k_ref, v_ref, do_ref, lse_ref, dq_ref, dk_ref, dv_ref, mask):
    for g in range(do_ref.shape[1] // GROUP):
        at = slice(GROUP * g, GROUP * g + GROUP)
        qs, dos = stacked(q_ref[:, at]), stacked(do_ref[:, at])
        k = k_ref[:, at]
        p = jnp.exp(mask(nt(k, qs)) - lse_ref[g : g + 1])
        dp = nt(v_ref[:, at], dos)
        ds = (p * (dp - jnp.sum(p * dp, axis=0, keepdims=True))).astype(BF)
        dv_ref[:, at] = nn(p.astype(BF), dos).astype(BF)
        dk_ref[:, at] = nn(ds, qs).astype(BF)
        dq_ref[:, at] = (unstacked(tn(ds, k)) * HEAD_DIM**-0.5).astype(BF)


def whole(shape):
    return pl.BlockSpec(shape, lambda *_: (0,) * len(shape), pipeline_mode=pl.Buffered(1))


def params(n=1):
    return pltpu.CompilerParams(
        dimension_semantics=("arbitrary",) * n, vmem_limit_bytes=LIMIT
    )


def cost(us):
    return pl.CostEstimate(flops=int(us * 1.1e9), bytes_accessed=int(us * 1e5), transcendentals=0)


def spatial_body(places, x, w, wo, vec, *refs):
    stream, n1, q, k, v, o, lse = refs[-7:]
    xv = x[0].astype(F32)
    d = xv.shape[1]
    n0 = (hat_of(xv)[0] * vec[0:1] + vec[1:2]).astype(BF)
    q[0] = ((nt(n0, w[0:d]) + vec[2:3]) * HEAD_DIM**-0.5).astype(BF)
    k[0] = nt(n0, w[d : 2 * d]).astype(BF)
    v[0] = (nt(n0, w[2 * d : 3 * d]) + vec[3:4]).astype(BF)
    attend(q.at[0], k.at[0], v.at[0], o.at[0], lse.at[0], only_places(places))
    s1 = xv + (nn(o[0], wo[...]) + vec[4:5])
    stream[0] = s1
    n1[0] = (hat_of(s1)[0] * vec[5:6] + vec[6:7]).astype(BF)


def spatial(x, w, wo, vec, places, frames, start, before=()):
    f, r, d = x.shape
    blk = pl.BlockSpec((1, r, d), lambda i: (i, 0, 0))
    out = pl.BlockSpec((1, r, d), lambda i: (i + start, 0, 0))
    big = jax.ShapeDtypeStruct((frames, r, d), BF)
    return pl.pallas_call(
        functools.partial(spatial_body, places),
        grid=(f,),
        in_specs=[blk, whole(w.shape), whole(wo.shape), whole(vec.shape)]
        + [pl.BlockSpec(memory_space=pl.ANY)] * len(before),
        out_specs=[out] * 6
        + [pl.BlockSpec((1, d // GROUP, PER * r), lambda i: (i + start, 0, 0))],
        out_shape=[jax.ShapeDtypeStruct((frames, r, d), F32)]
        + [big] * 5
        + [jax.ShapeDtypeStruct((frames, d // GROUP, PER * r), F32)],
        input_output_aliases={4 + i: i for i in range(len(before))},
        compiler_params=params(),
        name="spatial",
        cost_estimate=cost(3.6 * f),
    )(x, w, wo, vec, *before)


def temporal_body(n1, w, vec, q, k, v, o, lse):
    n = n1[0]
    d = n.shape[1]
    q[0] = ((nt(n, w[0:d]) + vec[0:1]) * HEAD_DIM**-0.5).astype(BF)
    k[0] = nt(n, w[d : 2 * d]).astype(BF)
    v[0] = (nt(n, w[2 * d : 3 * d]) + vec[1:2]).astype(BF)
    attend(q.at[0], k.at[0], v.at[0], o.at[0], lse.at[0], same_place(place_bias(n.shape[0])))


def temporal(n1, w, vec):
    b, r, d = n1.shape
    blk = pl.BlockSpec((1, r, d), lambda i: (i, 0, 0))
    return pl.pallas_call(
        temporal_body,
        grid=(b,),
        in_specs=[blk, whole(w.shape), whole(vec.shape)],
        out_specs=[blk] * 4 + [pl.BlockSpec((1, d // GROUP, PER * r), lambda i: (i, 0, 0))],
        out_shape=[jax.ShapeDtypeStruct((b, r, d), BF)] * 4
        + [jax.ShapeDtypeStruct((b, d // GROUP, PER * r), F32)],
        compiler_params=params(),
        name="temporal",
        cost_estimate=cost(2.4 * b),
    )(n1, w, vec)


def temporal_back_body(g, q, k, v, lse, w, wo, dn, dqkv, do):
    i = pl.program_id(0)
    d = g.shape[-1]
    r = q.shape[1]
    do[...] = nt(g[0], wo[...]).astype(BF)
    attend_back(
        q.at[0], k.at[0], v.at[0], do, lse.at[0],
        dqkv.at[0, i], dqkv.at[1, i], dqkv.at[2, i], same_place(place_bias(r)),
    )

    @pl.when(i == pl.num_programs(0) - 1)
    def _():
        rows = dqkv.shape[1] * r
        acc = nn(dqkv[0].reshape(rows, d), w[0:d])
        acc += nn(dqkv[1].reshape(rows, d), w[d : 2 * d])
        acc += nn(dqkv[2].reshape(rows, d), w[2 * d : 3 * d])
        dn[...] = acc.astype(BF).reshape(dn.shape)


def temporal_back(g, q, k, v, lse, w, wo):
    b, r, d = g.shape
    blk = pl.BlockSpec((1, r, d), lambda i: (i, 0, 0))
    return pl.pallas_call(
        temporal_back_body,
        grid=(b,),
        in_specs=[blk] * 4
        + [pl.BlockSpec((1, d // GROUP, PER * r), lambda i: (i, 0, 0)),
           whole(w.shape), whole(wo.shape)],
        out_specs=[whole(g.shape), whole((3, b, r, d))],
        out_shape=[jax.ShapeDtypeStruct(g.shape, BF), jax.ShapeDtypeStruct((3, b, r, d), BF)],
        scratch_shapes=[pltpu.VMEM((r, d), BF)],
        compiler_params=params(),
        name="temporal_back",
        cost_estimate=cost(36),
    )(g, q, k, v, lse, w, wo)


def weight_grads_body(dqkv, o, n, g, send, keep, sums):
    c = pl.program_id(0)
    d = n.shape[1]
    e = d // 4

    def put(m):
        m = m.astype(BF)
        for r in range(4):
            to = send if r % 2 else keep
            to[r // 2, 0] = m[r * e : (r + 1) * e]

    @pl.when(c < 3)
    def _():
        v = dqkv[0]
        put(tn(v, n[...]))
        sums[0] = jnp.sum(v.astype(F32), axis=0, keepdims=True)

    @pl.when(c == 3)
    def _():
        put(tn(o[...], g[...]))
        sums[0] = jnp.zeros_like(sums[0])


def weight_grads(dqkv, o, n, g):
    d = n.shape[-1]
    rows = n.size // d
    dqkv = dqkv.reshape(3, rows, d)
    o, n, g = (v.reshape(rows, d) for v in (o, n, g))
    out = pl.BlockSpec((2, 1, d // 4, d), lambda c: (0, c, 0, 0))
    return pl.pallas_call(
        weight_grads_body,
        grid=(4,),
        in_specs=[pl.BlockSpec((1, rows, d), lambda c: (jnp.minimum(c, 2), 0, 0))]
        + [whole((rows, d))] * 3,
        out_specs=[out, out, pl.BlockSpec((1, 1, d), lambda c: (c, 0, 0))],
        out_shape=[jax.ShapeDtypeStruct((2, 4, d // 4, d), BF)] * 2
        + [jax.ShapeDtypeStruct((4, 1, d), F32)],
        compiler_params=params(),
        name="weight_grads",
        cost_estimate=cost(14),
    )(dqkv, o, n, g)


def spatial_back_body(places, x, s1, dn1, g2, q, k, v, lse, w, wo, vec, *refs):
    g0, sums, dqkv, n0, gb, do = refs[-6:]
    i = pl.program_id(0)
    r, d = x.shape[1:]

    @pl.when(i == 0)
    def _():
        sums[...] = jnp.zeros_like(sums)

    def add(at, val):
        sums[at : at + 1] += jnp.sum(val, axis=0, keepdims=True)

    hat, inv = hat_of(s1[0])
    dn = dn1[0].astype(F32)
    add(2, dn * hat)
    add(3, dn)
    g1 = g2[0] + hat_back(hat, inv, vec[2:3], dn)
    add(4, g1)
    gb[0] = g1.astype(BF)
    do[...] = nt(gb[0], wo[...]).astype(BF)
    attend_back(
        q.at[0], k.at[0], v.at[0], do, lse.at[0],
        dqkv.at[0, 0], dqkv.at[1, 0], dqkv.at[2, 0], only_places(places),
    )
    hat, inv = hat_of(x[0].astype(F32))
    n0[0] = (hat * vec[0:1] + vec[1:2]).astype(BF)
    dn = nn(dqkv[0, 0], w[0:d]) + nn(dqkv[1, 0], w[d : 2 * d]) + nn(dqkv[2, 0], w[2 * d : 3 * d])
    add(0, dn * hat)
    add(1, dn)
    g0[0] = (g1 + hat_back(hat, inv, vec[0:1], dn)).astype(g0.dtype)


def spatial_back(x, s1, dn1, g2, q, k, v, lse, w, wo, vec, places, start, kind, before=()):
    f, r, d = x.shape
    frames = s1.shape[0]
    own = pl.BlockSpec((1, r, d), lambda i: (i, 0, 0))
    blk = pl.BlockSpec((1, r, d), lambda i: (i + start, 0, 0))
    big = jax.ShapeDtypeStruct((frames, r, d), BF)
    return pl.pallas_call(
        functools.partial(spatial_back_body, places),
        grid=(f,),
        in_specs=[own] + [blk] * 6
        + [pl.BlockSpec((1, d // GROUP, PER * r), lambda i: (i + start, 0, 0)),
           whole(w.shape), whole(wo.shape), whole(vec.shape)]
        + [pl.BlockSpec(memory_space=pl.ANY)] * len(before),
        out_specs=[own, whole((8, d)), pl.BlockSpec((3, 1, r, d), lambda i: (0, i + start, 0, 0)),
                   blk, blk],
        out_shape=[jax.ShapeDtypeStruct(x.shape, kind), jax.ShapeDtypeStruct((8, d), F32),
                   jax.ShapeDtypeStruct((3, frames, r, d), BF), big, big],
        input_output_aliases={11 + i: 2 + i for i in range(len(before))},
        scratch_shapes=[pltpu.VMEM((r, d), BF)],
        compiler_params=params(),
        name="spatial_back",
        cost_estimate=cost(5 * f),
    )(x, s1, dn1, g2, q, k, v, lse, w, wo, vec, *before)


def gelu_parts(u):
    cdf = 0.5 + 0.5 * lax.erf(u * 0.7071067811865476)
    return u * cdf, cdf + u * (jnp.exp(-0.5 * u * u) * 0.3989422804014327)


def mlp_step(n2, gb, wt, wd, b, s, branch, dn, gwt, gwd, gbi):
    u = nt(n2, wt[s]) + b[s]
    h, slope = gelu_parts(u)
    h = h.astype(BF)
    branch[...] += nn(h, wd[s])
    dr = (nt(gb, wd[s]) * slope).astype(BF)
    dn[...] += nn(dr, wt[s])
    gwt[s] += tn(dr, n2)
    gwd[s] += tn(h, gb)
    gbi[s] += jnp.sum(dr.astype(F32), axis=0, keepdims=True)


def mlp_ends(i, s, gwt, gwd, gbi, gwt_o, gwd_o):
    @pl.when(i == pl.num_programs(0) - 1)
    def _():
        gwt_o[s] = gwt[s].astype(BF)
        gwd_o[s] = gwd[s].astype(BF)


def mlp_first_body(s1, o1, gb, wo, vec, wt, wd, b, s2, n2, branch, dn, gwt_o, gwd_o, gbi, gwt, gwd):
    i, s = pl.program_id(0), pl.program_id(1)

    @pl.when((i == 0) & (s == 0))
    def _():
        gwt[...] = jnp.zeros_like(gwt)
        gwd[...] = jnp.zeros_like(gwd)
        gbi[...] = jnp.zeros_like(gbi)

    @pl.when(s == 0)
    def _():
        v = s1[...] + (nn(o1[...], wo[...]) + vec[0:1])
        s2[...] = v
        n2[...] = (hat_of(v)[0] * vec[1:2] + vec[2:3]).astype(BF)
        branch[...] = jnp.zeros_like(branch)
        dn[...] = jnp.zeros_like(dn)

    mlp_step(n2[...], gb[...], wt, wd, b, s, branch, dn, gwt, gwd, gbi)
    mlp_ends(i, s, gwt, gwd, gbi, gwt_o, gwd_o)


def mlp_first(s1, o1, gb, wo, vec, wt, wd, b, tile):
    rows, d = s1.shape
    ns, h, _ = wt.shape
    blk = pl.BlockSpec((tile, d), lambda i, s: (i, 0))
    sh = lambda t: jax.ShapeDtypeStruct((rows, d), t)
    return pl.pallas_call(
        mlp_first_body,
        grid=(rows // tile, ns),
        in_specs=[blk, blk, blk, whole(wo.shape), whole(vec.shape), whole(wt.shape),
                  whole(wd.shape), whole(b.shape)],
        out_specs=[blk] * 4 + [whole(wt.shape), whole(wd.shape), whole(b.shape)],
        out_shape=[sh(F32), sh(BF), sh(F32), sh(F32), jax.ShapeDtypeStruct(wt.shape, BF),
                   jax.ShapeDtypeStruct(wd.shape, BF), jax.ShapeDtypeStruct(b.shape, F32)],
        scratch_shapes=[pltpu.VMEM(wt.shape, F32), pltpu.VMEM(wd.shape, F32)],
        compiler_params=params(2),
        name="mlp_first",
        cost_estimate=cost(42),
    )(s1, o1, gb, wo, vec, wt, wd, b)


def mlp_second_body(s2, n2, gb, br0, dn0, vec, wt, wd, b,
                    near, far, g2, g2b, gwt_o, gwd_o, gbi, sums, branch, dn, gwt, gwd):
    i, s = pl.program_id(0), pl.program_id(1)

    @pl.when((i == 0) & (s == 0))
    def _():
        gwt[...] = jnp.zeros_like(gwt)
        gwd[...] = jnp.zeros_like(gwd)
        gbi[...] = jnp.zeros_like(gbi)
        sums[...] = jnp.zeros_like(sums)

    @pl.when(s == 0)
    def _():
        branch[...] = br0[...]
        dn[...] = dn0[...]

    mlp_step(n2[...], gb[...], wt, wd, b, s, branch, dn, gwt, gwd, gbi)
    mlp_ends(i, s, gwt, gwd, gbi, gwt_o, gwd_o)

    @pl.when(s == pl.num_programs(1) - 1)
    def _():
        def add(at, val):
            sums[at : at + 1] += jnp.sum(val, axis=0, keepdims=True)

        v = s2[...]
        out = v + (branch[...] + vec[0:1])

        @pl.when(i < pl.num_programs(0) // 2)
        def _():
            near[...] = out

        @pl.when(i >= pl.num_programs(0) // 2)
        def _():
            far[...] = out.astype(BF)

        hat, inv = hat_of(v)
        dv = dn[...]
        add(0, dv * hat)
        add(1, dv)
        g3 = gb[...].astype(F32)
        add(3, g3)
        g = g3 + hat_back(hat, inv, vec[1:2], dv)
        add(2, g)
        g2[...] = g
        g2b[...] = g.astype(BF)


def mlp_second(s2, n2, gb, br0, dn0, vec, wt, wd, b, tile):
    rows, d = s2.shape
    ns, h, _ = wt.shape
    half = rows // tile // 2
    blk = pl.BlockSpec((tile, d), lambda i, s: (i, 0))
    sh = lambda t, n=rows: jax.ShapeDtypeStruct((n, d), t)
    return pl.pallas_call(
        mlp_second_body,
        grid=(rows // tile, ns),
        in_specs=[blk] * 5 + [whole(vec.shape), whole(wt.shape), whole(wd.shape), whole(b.shape)],
        out_specs=[pl.BlockSpec((tile, d), lambda i, s: (jnp.minimum(i, half - 1), 0)),
                   pl.BlockSpec((tile, d), lambda i, s: (jnp.maximum(i - half, 0), 0)),
                   blk, blk, whole(wt.shape), whole(wd.shape), whole(b.shape), whole((8, d))],
        out_shape=[sh(F32, rows // 2), sh(BF, rows // 2), sh(F32), sh(BF),
                   jax.ShapeDtypeStruct(wt.shape, BF), jax.ShapeDtypeStruct(wd.shape, BF),
                   jax.ShapeDtypeStruct(b.shape, F32), jax.ShapeDtypeStruct((8, d), F32)],
        scratch_shapes=[pltpu.VMEM((tile, d), F32), pltpu.VMEM((tile, d), F32),
                        pltpu.VMEM(wt.shape, F32), pltpu.VMEM(wd.shape, F32)],
        compiler_params=params(2),
        name="mlp_second",
        cost_estimate=cost(42),
    )(s2, n2, gb, br0, dn0, vec, wt, wd, b)


def finish_body(dp, gs, gk, t1, rel, rep, f0, f1, rel_o, rep_o, *scratch):
    (rc, kk, ry, rx, tt, zr, ta, tb, aa, ab, xs, rel_r, rep_r, rel_s, rep_s, send, recv) = scratch
    me_d, me_t = lax.axis_index("dp"), lax.axis_index("tensor")
    x = lax.rem(me_d, 2)
    bits = []
    bit = 2
    while bit < dp:
        bits.append(bit)
        bit *= 2

    def flip(v, b):
        return v + b - 2 * b * lax.rem(v // b, 2)

    def core():
        return (me_d, flip(me_t, 1))

    def over_y():
        return (me_d, flip(me_t, 2))

    def over_d(b):
        return (flip(me_d, b), me_t)

    partners = [core(), over_y(), over_d(1)] + [over_d(b) for b in bits]
    barrier = pltpu.get_barrier_semaphore()
    for p in partners:
        pl.semaphore_signal(barrier, inc=1, device_id=p, device_id_type=pl.DeviceIdType.MESH)
    pl.semaphore_wait(barrier, len(partners))

    count = [0]

    def copy(src, dst, to):
        k = count[0]
        count[0] += 1
        c = pltpu.make_async_remote_copy(
            src_ref=src, dst_ref=dst, send_sem=send.at[k], recv_sem=recv.at[k],
            device_id=to, device_id_type=pl.DeviceIdType.MESH,
        )
        c.start()
        return c

    def plus(a, b):
        return (a.astype(F32) + b.astype(F32)).astype(BF)

    n = tt.shape[1]

    def rest(k, out):
        size, held = n, tt.at[k]
        done = []
        for z, b in enumerate(bits[:2]):
            half = size // 2
            bitv = lax.rem(me_d // b, 2)
            mine = pl.multiple_of(bitv * half, 16)
            other = pl.multiple_of((1 - bitv) * half, 16)
            dst = zr.at[k, z, pl.ds(0, half)]
            c = copy(held.at[pl.ds(other, half)], dst, over_d(b))
            yield
            c.wait()
            nxt = (ta if z == 0 else tb).at[k]
            nxt[...] = plus(held[pl.ds(mine, half)], dst[...])
            done.append(((aa if z == 0 else ab).at[k], mine, half, b))
            size, held = half, nxt
        for z, b in enumerate(bits[2:]):
            dst = zr.at[k, 2 + z, pl.ds(0, size)]
            c = copy(held, dst, over_d(b))
            yield
            c.wait()
            held[...] = plus(held[...], dst[...])
        for z, (up, mine, half, b) in enumerate(reversed(done)):
            up[pl.ds(mine, half)] = held[...]
            c = copy(up.at[pl.ds(mine, half)], up.at[pl.ds(mine, half)], over_d(b))
            yield
            c.wait()
            held = up
        c = copy(held, xs.at[k], over_d(1))
        yield
        c.wait()
        out(held, xs.at[k])

    def attn0(j):
        c = [copy(gs.at[:, j + 2 * u], rc.at[j, u], core()) for u in range(2)]
        yield
        for v in c:
            v.wait()
        for u in range(2):
            at = x + u - 2 * x * u
            for r in range(2):
                kk[j, u, r] = plus(gk[r, j + 2 * at], rc[j, at, r])
        if j == 0:
            c = [copy(kk.at[j, u, 1], ry.at[j, u], over_y()) for u in (1, 0)]
            yield
            c[0].wait()
            kk[j, 1, 0] = plus(kk[j, 1, 0], ry[j, 1])
            d = copy(kk.at[j, 1, 0], rx.at[j, 0], over_d(1))
            c[1].wait()
            kk[j, 0, 0] = plus(kk[j, 0, 0], ry[j, 0])
            yield
            d.wait()
            tt[j] = plus(kk[j, 0, 0], rx[j, 0])
        else:
            c = [copy(kk.at[j, 1, r], rx.at[j, r], over_d(1)) for r in (1, 0)]
            yield
            c[0].wait()
            kk[j, 0, 1] = plus(kk[j, 0, 1], rx[j, 1])
            d = copy(kk.at[j, 0, 1], ry.at[j, 0], over_y())
            c[1].wait()
            kk[j, 0, 0] = plus(kk[j, 0, 0], rx[j, 0])
            yield
            d.wait()
            tt[j] = plus(kk[j, 0, 0], ry[j, 0])

        def out(mine, got):
            f0[j + 2 * x] = mine[...]
            f0[j + 2 * (1 - x)] = got[...]

        yield from rest(j, out)

    def attn1(j):
        k = 2 + j
        tt[k] = t1[j]

        def out(mine, got):
            f1[j + 2 * x] = mine[...]
            f1[j + 2 * (1 - x)] = got[...]

        yield from rest(k, out)

    def small():
        rel_s[...] = rel[...]
        rep_s[...] = rep[...]
        for z, (to, b) in enumerate([(core(), 1), (over_y(), 2)]):
            c = [copy(rel_s, rel_r.at[z], to), copy(rep_s, rep_r.at[z], to)]
            yield
            for v in c:
                v.wait()
            rep_s[...] += rep_r[z]
            for r in range(4):
                rel_s[r] = rel_s[r] + rel_r[z, r ^ b]
        for z, b in enumerate([1] + bits):
            c = [
                copy(rel_s.at[0], rel_r.at[2 + z, 0], over_d(b)),
                copy(rep_s, rep_r.at[2 + z], over_d(b)),
            ]
            yield
            for v in c:
                v.wait()
            rep_s[...] += rep_r[2 + z]
            rel_s[0] = rel_s[0] + rel_r[2 + z, 0]
        rel_o[...] = rel_s[0]
        rep_o[...] = rep_s[...]

    chains = [attn0(0), attn0(1), attn1(0), attn1(1), small()]
    while chains:
        left = []
        for chain in chains:
            try:
                next(chain)
                left.append(chain)
            except StopIteration:
                pass
        chains = left


def finish(gs, gk, t1, rel, rep, dp):
    _, _, n, d = gs.shape
    nb = max(dp.bit_length() - 2, 0)
    vm = pl.BlockSpec(memory_space=pltpu.VMEM)
    return pl.pallas_call(
        functools.partial(finish_body, dp),
        in_specs=[vm] * 5,
        out_specs=[vm] * 4,
        out_shape=[jax.ShapeDtypeStruct((4, n, d), BF)] * 2
        + [jax.ShapeDtypeStruct(rel.shape[1:], F32), jax.ShapeDtypeStruct(rep.shape, F32)],
        scratch_shapes=[
            pltpu.VMEM((2, 2, 2, n, d), BF),
            pltpu.VMEM((2, 2, 2, n, d), BF),
            pltpu.VMEM((2, 2, n, d), BF),
            pltpu.VMEM((2, 2, n, d), BF),
            pltpu.VMEM((4, n, d), BF),
            pltpu.VMEM((4, max(nb, 1), n // 2, d), BF),
            pltpu.VMEM((4, n // 2, d), BF),
            pltpu.VMEM((4, n // 4, d), BF),
            pltpu.VMEM((4, n, d), BF),
            pltpu.VMEM((4, n // 2, d), BF),
            pltpu.VMEM((4, n, d), BF),
            pltpu.VMEM((3 + nb,) + rel.shape, F32),
            pltpu.VMEM((3 + nb,) + rep.shape, F32),
            pltpu.VMEM(rel.shape, F32),
            pltpu.VMEM(rep.shape, F32),
            pltpu.SemaphoreType.DMA((96,)),
            pltpu.SemaphoreType.DMA((96,)),
        ],
        compiler_params=pltpu.CompilerParams(
            collective_id=0, has_side_effects=True, vmem_limit_bytes=LIMIT
        ),
        name="finish",
        cost_estimate=cost(60),
    )(gs, gk, t1, rel, rep)


ROWS = 208
HALF = ROWS // 2
TILE = 416


def shards(clips, cot, gain, shift, qkv, qvb, wout, bout, win, b_in, wdown, bdown):
    tensor = lax.axis_index("tensor")
    y, core = tensor // 2, tensor % 2
    x = lax.axis_index("dp") % 2
    dp = lax.axis_size("dp")
    width = clips.shape[-1]
    places = clips.shape[2]
    e = qkv.shape[-1]
    h = win.shape[1] // 2

    def over_tensor(v, bit):
        return lax.ppermute(v, "tensor", [(i, i ^ bit) for i in range(4)])

    def over_dp(v, bit):
        return lax.ppermute(v, "dp", [(i, i ^ bit) for i in range(dp)])

    def after(v, *others):
        return lax.optimization_barrier((v,) + others)[0]

    def pad(v):
        return jnp.pad(v, ((0, 0), (0, ROWS - places), (0, 0)))

    def split(a, b):
        return jnp.where(x == 0, a, b), jnp.where(x == 0, b, a)

    def swap_clip(v):
        return over_tensor(lax.dynamic_index_in_dim(v, 1 - y, 0, False), 2)

    def mine_of(v):
        return lax.dynamic_index_in_dim(v, y, 0, False)

    def back(mine, got):
        mine, got = mine[:, :places], got[:, :places]
        return jnp.stack([jnp.where(y == 0, mine, got), jnp.where(y == 0, got, mine)])

    wt = [qkv[i].transpose(0, 2, 1).reshape(3 * e, width) for i in range(2)]
    pa = [v[: 2 * e] for v in wt]
    pb = [jnp.concatenate([v[2 * e :], wout[i]]) for i, v in enumerate(wt)]
    send = [jnp.where(x == 0, pa[i], pb[i]) for i in range(2)]
    y0 = over_tensor(send[0], 2)
    y1 = over_tensor(after(send[1], send[0]), 2)
    x_got = swap_clip(after(clips, send[0], send[1]))
    ab = [jnp.concatenate([pa[i], pb[i]]) for i in range(2)]
    c0 = over_tensor(ab[0], 1)
    bias = jnp.concatenate([qvb.reshape(1, -1), b_in.reshape(1, -1)])
    bias_y = over_tensor(bias, 2)
    bias_all = jnp.stack([bias, over_tensor(bias, 1), bias_y, over_tensor(bias_y, 1)])
    x0 = over_dp(y0, 1)
    cy0 = over_tensor(y0, 1)
    cx0 = over_tensor(x0, 1)
    win_t = win.T
    at = x * h
    send_m = [
        lax.dynamic_slice_in_dim(after(v, y0), at, h, 0) for v in (win_t, wdown)
    ]
    m_y = [over_tensor(v, 2) for v in send_m]
    cot_got = swap_clip(after(cot, x0, *send_m))
    x1 = over_dp(y1, 1)
    c1 = over_tensor(after(ab[1], c0), 1)
    cy1 = over_tensor(y1, 1)
    cx1 = over_tensor(x1, 1)
    m_x = [over_dp(v, 1) for v in m_y]
    m_c = [over_tensor(after(v, c0), 1) for v in (win_t, wdown)]
    m_cy = [over_tensor(v, 1) for v in m_y]
    m_cx = [over_tensor(v, 1) for v in m_x]

    def attn_weights(i, own, c, yy, xx, cy, cx):
        a2, b2 = split(yy, xx)
        a3, b3 = split(cy, cx)
        shards_a = [own[: 2 * e], c[: 2 * e], a2, a3]
        shards_b = [own[2 * e :], c[2 * e :], b2, b3]
        w = jnp.concatenate(
            [v[:e] for v in shards_a] + [v[e:] for v in shards_a] + [v[:e] for v in shards_b]
        )
        wo = jnp.concatenate([v[e:] for v in shards_b])
        b = bias_all[:, 0].reshape(4, 2, 2, e)
        return w, wo, b[:, i, 0].reshape(-1), b[:, i, 1].reshape(-1)

    def mlp_weights(k):
        two = jnp.concatenate(split(m_y[k], m_x[k]))
        three = jnp.concatenate(split(m_cy[k], m_cx[k]))
        own = (win_t, wdown)[k]
        return jnp.stack([three, m_c[k]]), jnp.stack([two, own])

    def to_places(v):
        own = lax.dynamic_slice_in_dim(v, HALF * core, HALF, 1)
        send = lax.dynamic_slice_in_dim(v, HALF * (1 - core), HALF, 1)
        both = jnp.concatenate([own, over_tensor(send, 1)])
        f = both.shape[0]
        both = both.reshape(f, HALF // 8, 8, width).transpose(1, 0, 2, 3)
        return both.reshape(HALF // 8, f * 8, width)

    def to_frames(v, flip=False):
        f = v.shape[1] // 8
        v = v.reshape(HALF // 8, f, 8, width).transpose(1, 0, 2, 3).reshape(f, HALF, width)
        own = v[: f // 2]
        got = over_tensor(v[f // 2 :], 1)
        if flip:
            got = jnp.concatenate([got[..., i * e : (i + 1) * e] for i in (1, 0, 3, 2)], axis=-1)
        return jnp.concatenate(
            [jnp.where(core == 0, own, got), jnp.where(core == 0, got, own)], axis=1
        )

    def rows8(*vs):
        return jnp.pad(jnp.stack(vs), ((0, 8 - len(vs)), (0, 0)))

    frames = 2 * clips.shape[1]
    flat = (frames * ROWS, width)
    w0, wo0, bq0, bv0 = attn_weights(0, ab[0], c0, y0, x0, cy0, cx0)
    w1, wo1, bq1, bv1 = attn_weights(1, ab[1], c1, y1, x1, cy1, cx1)
    vec = rows8(gain[0], shift[0], bq0, bv0, bout[0], gain[1], shift[1])
    xs = [pad(mine_of(clips)), pad(x_got)]
    half = frames // 2
    fwd = spatial(xs[0], w0, wo0, vec, places, frames, 0)
    s1, n1, q0, k0, v0, o0, lse0 = spatial(xs[1], w0, wo0, vec, places, frames, half, fwd)
    n1p = to_places(n1)
    q1, k1, v1, o1p, lse1 = temporal(n1p, w1, rows8(bq1, bv1))
    o1 = to_frames(o1p, True)
    wts, wds = mlp_weights(0), mlp_weights(1)
    bm = bias_all[:, 1:2]
    ma = (wts[0], wds[0], jnp.stack([bm[3], bm[1]]))
    mb = (wts[1], wds[1], jnp.stack([bm[2], bm[0]]))
    gb3 = jnp.concatenate([pad(mine_of(cot)), pad(cot_got)]).reshape(flat)

    vec = rows8(bout[1], gain[2], shift[2])
    s2, n2, branch, dn2, gwt_a, gwd_a, gb_a = mlp_first(
        s1.reshape(flat), o1.reshape(flat), gb3, wo1, vec, *ma, TILE
    )
    near, far, g2, g2b, gwt_b, gwd_b, gb_b, sums2 = mlp_second(
        s2, n2, gb3, branch, dn2, rows8(bdown, gain[2]), *mb, TILE
    )
    shape3 = (frames, ROWS, width)
    shape2 = (half, ROWS, width)

    def pick(v, axis):
        n = v.shape[axis] // 2
        return (
            lax.dynamic_slice_in_dim(v, x * n, n, axis),
            lax.dynamic_slice_in_dim(v, (1 - x) * n, n, axis),
        )

    keep_t = gwt_b + over_tensor(gwt_a, 1)
    keep_d = gwd_b + over_tensor(gwd_a, 1)
    g2p = to_places(g2b.reshape(shape3))
    g2p, keep_t, keep_d = lax.optimization_barrier((g2p, keep_t, keep_d))
    got_t = over_tensor(keep_t[0], 2)
    mine_d, send_d = pick(keep_d, 1)
    got_d = over_dp(send_d, 1)
    far_got = over_tensor(after(far.reshape(shape2)[:, :places], keep_t), 2)

    dn1p, dqkv1 = temporal_back(g2p, q1, k1, v1, lse1, w1, wo1)
    mine_t, send_t = pick(keep_t[1] + got_t, 0)
    mine_d = mine_d + got_d
    dn1 = to_frames(dn1p)
    gs1, gk1, sums1 = weight_grads(dqkv1, o1p, n1p, g2p)
    dn1, mine_t, send_t, mine_d = lax.optimization_barrier((dn1, mine_t, send_t, mine_d))
    got_t = over_dp(send_t, 1)
    got_d = over_tensor(mine_d[0], 2)
    keep1 = gk1 + over_tensor(gs1, 1)
    dn1, keep1 = lax.optimization_barrier((dn1, keep1))
    mine1, send1 = pick(keep1, 1)
    got1 = over_dp(send1, 1)
    output = back(near.reshape(shape2), far_got.astype(F32))
    g2 = g2.reshape(shape3)
    vec = rows8(gain[0], shift[0], gain[1])
    kept = (s1, dn1, g2, q0, k0, v0, lse0, w0, wo0, vec, places)
    g0_far, sums_f, *rest = spatial_back(xs[1], *kept, half, BF)
    in_got = over_tensor(g0_far[:, :places], 2)
    mlp_sum = jnp.concatenate([mine_t + got_t, mine_d[1] + got_d])
    mine1 = mine1 + got1
    rest[0], mlp_sum, mine1 = lax.optimization_barrier((rest[0], mlp_sum, mine1))
    if dp > 2:
        groups = [[i for i in range(dp) if i % 2 == p] for p in range(2)]
        mlp_sum = lax.psum(mlp_sum, "dp", axis_index_groups=groups)
    got1 = over_tensor(mine1[1], 2)
    g0, sums_n, dqkv0, n0, gb0 = spatial_back(xs[0], *kept, 0, F32, rest)
    t1 = mine1[0] + got1
    sums0 = sums_f + sums_n
    gs0, gk0, sums_b = weight_grads(dqkv0, o0, n0, gb0)
    input_grad = back(g0, in_got.astype(F32))

    rep = jnp.stack(
        [sums0[0], sums0[2], sums2[0], sums0[1], sums0[3], sums2[1], sums0[4], sums2[2], sums2[3]]
    )
    rep = jnp.pad(rep, ((0, 7), (0, 0)))
    qv = jnp.stack([sums_b[0, 0], sums_b[2, 0], sums1[0, 0], sums1[2, 0]])
    qv = qv.reshape(4, 4, e).transpose(1, 0, 2).reshape(4, 1, 4 * e)
    hid = jnp.stack([gb_b[1], gb_a[1], gb_b[0], gb_a[0]])
    rel = jnp.concatenate([qv, hid, jnp.zeros((4, 6, width), F32)], axis=1)
    f0, f1, rel, rep = finish(gs0, gk0, t1, rel, rep, dp)
    mlp = split(mlp_sum, over_dp(mlp_sum, 1))

    gqkv = jnp.stack([f0[:3], f1[:3]]).astype(F32).transpose(0, 1, 3, 2)
    gout = jnp.stack([f0[3], f1[3]]).astype(F32)
    gqv = rel[0].reshape(2, 2, e)
    gwin = jnp.concatenate([v[:h] for v in mlp]).T.astype(F32)
    gwd = jnp.concatenate([v[h:] for v in mlp]).astype(F32)
    return (
        output,
        input_grad,
        rep[0:3],
        rep[3:6],
        gqkv,
        gqv,
        gout,
        rep[6:8],
        gwin,
        rel[1],
        gwd,
        rep[8],
    )


def solution(mesh):
    placed = (
        P("dp", "tensor", None, None),
        P("dp", "tensor", None, None),
        P(),
        P(),
        P(None, None, None, "tensor"),
        P(None, None, "tensor"),
        P(None, "tensor", None),
        P(),
        P(None, "tensor"),
        P("tensor"),
        P("tensor", None),
        P(),
    )
    return jax.shard_map(
        shards,
        mesh=mesh,
        in_specs=placed,
        out_specs=(
            P("dp", "tensor", None, None),
            P("dp", "tensor", None, None),
            P(),
            P(),
            P(None, None, None, "tensor"),
            P(None, None, "tensor"),
            P(None, "tensor", None),
            P(),
            P(None, "tensor"),
            P("tensor"),
            P("tensor", None),
            P(),
        ),
        check_vma=False,
    )
```

```python
import functools

import jax
import jax.numpy as jnp
from jax import lax
from jax.experimental import pallas as pl
from jax.experimental.pallas import tpu as pltpu
from jax.sharding import PartitionSpec as P

BF = jnp.bfloat16
F32 = jnp.float32
HEAD_DIM = 64
norm_epsilon = 1e-06
LIMIT = 60 << 20
ROWS = 208
HALF = ROWS // 2


def nn(a, b):
    return lax.dot_general(a, b, (((1,), (0,)), ((), ())), preferred_element_type=F32)


def nt(a, b):
    return lax.dot_general(a, b, (((1,), (1,)), ((), ())), preferred_element_type=F32)


def tn(a, b):
    return lax.dot_general(a, b, (((0,), (0,)), ((), ())), preferred_element_type=F32)


def hat_of(values):
    mean = jnp.mean(values, axis=-1, keepdims=True)
    centered = values - mean
    inv = lax.rsqrt(jnp.mean(centered * centered, axis=-1, keepdims=True) + norm_epsilon)
    return centered * inv, inv


def hat_back(hat, inv, gain, grad):
    e = grad * gain
    return inv * (
        e - jnp.mean(e, axis=-1, keepdims=True) - hat * jnp.mean(e * hat, axis=-1, keepdims=True)
    )


GROUP = 256
PER = GROUP // HEAD_DIM


def head_of_lane(rows):
    return lax.broadcasted_iota(jnp.int32, (rows, GROUP), 1) // HEAD_DIM


def stacked(v):
    lane = head_of_lane(v.shape[0])
    return jnp.concatenate([jnp.where(lane == h, v, jnp.zeros_like(v)) for h in range(PER)])


def unstacked(v):
    rows = v.shape[0] // PER
    lane = head_of_lane(rows)
    out = v[:rows]
    for h in range(1, PER):
        out = jnp.where(lane == h, v[h * rows : (h + 1) * rows], out)
    return out


def only_places(places):
    def mask(s):
        cut = places // 8 * 8
        row = lax.broadcasted_iota(jnp.int32, (s.shape[0] - cut, s.shape[1]), 0)
        return jnp.concatenate([s[:cut], jnp.where(row < places - cut, s[cut:], -1e30)])

    return mask


def same_place(bias):
    return lambda s: s + bias


def place_bias(rows):
    a = lax.broadcasted_iota(jnp.int32, (rows, PER * rows), 0) & 7
    b = lax.broadcasted_iota(jnp.int32, (rows, PER * rows), 1) & 7
    return jnp.where(a == b, 0.0, -1e30).astype(F32)


def attend(q, k, v, o, lse, mask):
    spans = [slice(a, a + GROUP) for a in range(0, q.shape[1], GROUP)]
    s = [mask(nt(k[:, at], stacked(q[:, at]))) for at in spans]
    top = [jnp.max(m, axis=0, keepdims=True) for m in s]
    ex = [jnp.exp(m - t) for m, t in zip(s, top)]
    total = [jnp.sum(m, axis=0, keepdims=True) for m in ex]
    p = [(m * (1.0 / t)).astype(BF) for m, t in zip(ex, total)]
    r = [tn(m, v[:, at]) for m, at in zip(p, spans)]
    for g, at in enumerate(spans):
        o(at, unstacked(r[g]))
        lse[g : g + 1] = top[g] + jnp.log(total[g])


def attend_back(q, k, v, do, lse, dq, dk, dv, mask):
    spans = [slice(a, a + GROUP) for a in range(0, q.shape[1], GROUP)]
    qs = [stacked(q[:, at]) for at in spans]
    dos = [stacked(do[:, at]) for at in spans]
    s = [mask(nt(k[:, at], m)) for at, m in zip(spans, qs)]
    dp = [nt(v[:, at], m) for at, m in zip(spans, dos)]
    p = [jnp.exp(m - lse[g : g + 1]) for g, m in enumerate(s)]
    row = [jnp.sum(a * b, axis=0, keepdims=True) for a, b in zip(p, dp)]
    ds = [(a * (b - t)).astype(BF) for a, b, t in zip(p, dp, row)]
    for g, at in enumerate(spans):
        dv[:, at] = nn(p[g].astype(BF), dos[g]).astype(BF)
        dk[:, at] = nn(ds[g], qs[g]).astype(BF)
    r = [tn(m, k[:, at]) for m, at in zip(ds, spans)]
    for g, at in enumerate(spans):
        dq[:, at] = (unstacked(r[g]) * HEAD_DIM**-0.5).astype(BF)


def whole(shape, index=None):
    index = (0,) * len(shape) if index is None else index
    return pl.BlockSpec(shape, lambda *_: index, pipeline_mode=pl.Buffered(1))


def cost(us):
    return pl.CostEstimate(flops=int(us * 1.1e9), bytes_accessed=int(us * 1e5), transcendentals=0)


def struct(shape, kind):
    return jax.ShapeDtypeStruct(shape, kind)


ANY = pl.BlockSpec(memory_space=pl.ANY)
MESH = pl.DeviceIdType.MESH


def call(body, name, us, ids, grid, in_specs, out_specs, out_shape, args, scratch=(), aliases=None):
    return pl.pallas_call(
        body,
        grid_spec=pltpu.PrefetchScalarGridSpec(
            num_scalar_prefetch=1,
            grid=grid,
            in_specs=in_specs,
            out_specs=out_specs,
            scratch_shapes=list(scratch),
        ),
        out_shape=out_shape,
        input_output_aliases=aliases or {},
        compiler_params=pltpu.CompilerParams(
            dimension_semantics=("arbitrary",) * len(grid), vmem_limit_bytes=LIMIT
        ),
        name=name,
        cost_estimate=cost(us),
    )(ids, *args)


def core_index():
    return lax.rem(lax.axis_index("tensor"), 2)


def joined(own, got):
    first = core_index() == 0
    a, b = own.astype(F32), got.astype(F32)
    return jnp.concatenate([jnp.where(first, a, b), jnp.where(first, b, a)], axis=-2)


def parted(v, own, send):
    first = core_index() == 0
    n = v.shape[1] // 2
    a, b = v[:, :n], v[:, n:]
    own[...] = jnp.where(first, a, b).astype(BF)
    send[...] = jnp.where(first, b, a).astype(BF)


def in_blocks(own, got, out):
    f, blocks, _, d = own.shape
    for b in range(blocks):
        both = [v[:, b].astype(F32).reshape(f * 8, d) for v in (own, got)]
        out[b] = jnp.concatenate(both).astype(BF)


def start_body(qkv, wout, bias, clips, w, far, b, own, send, recv, local):
    me_d, me_t = lax.axis_index("dp"), lax.axis_index("tensor")
    x, y = lax.rem(me_d, 2), me_t // 2
    core = (me_d, me_t + 1 - 2 * lax.rem(me_t, 2))
    over_y = (me_d, me_t + 2 - 4 * y)
    over_x = (me_d + 1 - 2 * x, me_t)
    z = lax.rem(me_d // 2, 2)
    over_z = (me_d + 2 - 4 * z, me_t)
    loads = []
    for i in range(2):
        loads.append(pltpu.make_async_copy(qkv.at[i], own.at[i, 0:3], local.at[3 * i]))
        loads.append(pltpu.make_async_copy(wout.at[i], own.at[i, 3], local.at[3 * i + 1]))
    for c in loads:
        c.start()
    barrier = pltpu.get_barrier_semaphore()
    for to in (core, over_y, over_x, over_z):
        pl.semaphore_signal(barrier, inc=1, device_id=to, device_id_type=MESH)
    pl.semaphore_wait(barrier, 4)
    count = [0]

    def copy(src, dst, to):
        k = count[0]
        count[0] += 1
        c = pltpu.make_async_remote_copy(
            src_ref=src, dst_ref=dst, send_sem=send.at[k], recv_sem=recv.at[k],
            device_id=to, device_id_type=MESH,
        )
        c.start()
        return c

    one, two = 2 * x + z, 2 * x + 1 - z
    mine, other = pl.ds(2 * x, 2), pl.ds(2 - 2 * x, 2)
    done, ys, zs, xs = [], [], [], []
    for i in range(2):
        loads[2 * i].wait()
        loads[2 * i + 1].wait()
        ys.append(copy(own.at[i, one], w.at[i, one, 2], over_y))
    done.append(copy(clips.at[1 - y], far, over_y))
    for i in range(2):
        done.append(copy(own.at[i], w.at[i, :, 1], core))
        c = pltpu.make_async_copy(own.at[i], w.at[i, :, 0], local.at[3 * i + 2])
        c.start()
        done.append(c)
    b[0] = bias[...]
    done.append(copy(b.at[0], b.at[1], core))
    by = copy(b.at[0], b.at[2], over_y)
    for i in range(2):
        ys[i].wait()
        zs.append(copy(w.at[i, one, 2], w.at[i, one, 2], over_z))
        done.append(copy(w.at[i, one, 2], w.at[i, one, 3], core))
    for i in range(2):
        zs[i].wait()
        xs.append(copy(w.at[i, mine, 2], w.at[i, mine, 2], over_x))
        done.append(copy(w.at[i, two, 2], w.at[i, two, 3], core))
    for i in range(2):
        xs[i].wait()
        done.append(copy(w.at[i, other, 2], w.at[i, other, 3], core))
    by.wait()
    done.append(copy(b.at[2], b.at[3], core))
    for c in done:
        c.wait()


def start(qkv, wout, bias, clips):
    _, _, e, d = qkv.shape
    return pl.pallas_call(
        start_body,
        in_specs=[ANY, ANY, pl.BlockSpec(memory_space=pltpu.VMEM), ANY],
        out_specs=[ANY, ANY, pl.BlockSpec(memory_space=pltpu.VMEM)],
        out_shape=[struct((2, 4, 4, e, d), BF), struct(clips.shape[1:], BF),
                   struct((4,) + bias.shape, F32)],
        scratch_shapes=[pltpu.VMEM((2, 4, e, d), BF), pltpu.SemaphoreType.DMA((20,)),
                        pltpu.SemaphoreType.DMA((20,)), pltpu.SemaphoreType.DMA((6,))],
        compiler_params=pltpu.CompilerParams(
            collective_id=1, has_side_effects=True, vmem_limit_bytes=LIMIT
        ),
        name="start",
        cost_estimate=cost(50),
    )(qkv, wout, bias, clips)


def weight(w, c):
    v = w[0, c]
    return v.reshape(v.shape[0] * v.shape[1], v.shape[2])


def spatial_body(ids, x, w, gain, shift, qv, bout, *refs):
    stream, n_own, n_send, q, k, v, o, lse, rows = refs[-9:]
    f, r, d = rows.shape
    places = x.shape[-2]

    @pl.when(pl.program_id(0) == 0)
    def _():
        rows[...] = jnp.zeros_like(rows)

    rows[:, :places] = x[...].reshape(f, places, d).astype(F32)
    xv = rows[...].reshape(f * r, d)
    n0 = (hat_of(xv)[0] * gain[0:1] + shift[0:1]).astype(BF)

    def three(m):
        return m.astype(BF).reshape(f, r, d)

    q[...] = three((nt(n0, weight(w, 0)) + qv[0:1]) * HEAD_DIM**-0.5)
    k[...] = three(nt(n0, weight(w, 1)))
    v[...] = three(nt(n0, weight(w, 2)) + qv[1:2])
    for j in range(f):

        def put(at, m, j=j):
            o[j, :, at] = m.astype(BF)

        attend(q.at[j], k.at[j], v.at[j], put, lse.at[j], only_places(places))
    s1 = xv + (nn(o[...].reshape(f * r, d), weight(w, 3)) + bout[0:1])
    stream[...] = s1.reshape(f, r, d)
    n1 = hat_of(s1)[0] * gain[1:2] + shift[1:2]
    parted(n1.reshape(f, r, d), n_own, n_send)


def tokens_spec(near, places, d):
    if near:
        return pl.BlockSpec((1, 2, places, d), lambda i, t: (t[0], i, 0, 0))
    return pl.BlockSpec((2, places, d), lambda i, t: (i, 0, 0))


def spatial(ids, x, w, gain, shift, qv, bout, near, before=()):
    n, places, d = x.shape[-3:]
    steps, frames = n // 2, 2 * n
    begin = 0 if near else steps
    blk = pl.BlockSpec((2, ROWS, d), lambda i, t: (i + begin, 0, 0))
    part = pl.BlockSpec((2, HALF, d), lambda i, t: (i + begin, 0, 0))
    return call(
        spatial_body, "spatial", 12, ids, (steps,),
        [tokens_spec(near, places, d), whole((1,) + w.shape[1:]), whole(gain.shape),
         whole(shift.shape), whole(qv.shape), whole(bout.shape)] + [ANY] * len(before),
        [blk, part, part] + [blk] * 4
        + [pl.BlockSpec((2, d // GROUP, PER * ROWS), lambda i, t: (i + begin, 0, 0))],
        [struct((frames, ROWS, d), F32)] + [struct((frames, HALF, d), BF)] * 2
        + [struct((frames, ROWS, d), BF)] * 4
        + [struct((frames, d // GROUP, PER * ROWS), F32)],
        (x, w, gain, shift, qv, bout) + tuple(before),
        [pltpu.VMEM((2, ROWS, d), F32)],
        {7 + i: i for i in range(len(before))},
    )


def temporal_body(ids, own, got, w, qv, n, q, k, v, o, o_own, o_send, lse):
    i = pl.program_id(0)
    b, r, d = n.shape
    f = own.shape[0]

    @pl.when(i == 0)
    def _():
        in_blocks(own, got, n)
        step = b * r // 4
        ws = [weight(w, c) for c in range(3)]
        for c in range(4):
            at = slice(c * step, (c + 1) * step)
            t = n[...].reshape(b * r, d)[at]
            q[at] = ((nt(t, ws[0]) + qv[2:3]) * HEAD_DIM**-0.5).astype(BF)
            k[at] = nt(t, ws[1]).astype(BF)
            v[at] = (nt(t, ws[2]) + qv[3:4]).astype(BF)

    at = pl.ds(pl.multiple_of(i * r, r), r)

    def put(lanes, m):
        o[0, :, lanes] = m.astype(BF)
        m = m.reshape(2 * f, 1, 8, GROUP)
        o_own[:, :, :, lanes] = m[:f].astype(BF)
        o_send[:, :, :, lanes] = m[f:].astype(BF)

    attend(q.at[at], k.at[at], v.at[at], put, lse.at[0], same_place(place_bias(r)))


def temporal(ids, own, got, w, qv):
    f, half, d = own.shape
    b, r = half // 8, 16 * f
    own, got = own.reshape(f, b, 8, d), got.reshape(f, b, 8, d)
    part = pl.BlockSpec((f, 1, 8, d), lambda i, t: (0, i, 0, 0))
    res = call(
        temporal_body, "temporal", 22, ids, (b,),
        [whole(own.shape), whole(got.shape), whole((1,) + w.shape[1:], (1, 0, 0, 0, 0)),
         whole(qv.shape)],
        [whole((b, r, d))] + [whole((b * r, d))] * 3
        + [pl.BlockSpec((1, r, d), lambda i, t: (i, 0, 0)), part, part,
           pl.BlockSpec((1, d // GROUP, PER * r), lambda i, t: (i, 0, 0))],
        [struct((b, r, d), BF)] + [struct((b * r, d), BF)] * 3 + [struct((b, r, d), BF)]
        + [struct(own.shape, BF)] * 2 + [struct((b, d // GROUP, PER * r), F32)],
        (own, got, w, qv),
    )
    n, q, k, v, o, o_own, o_send, lse = res
    return n, q, k, v, o, o_own.reshape(f, half, d), o_send.reshape(f, half, d), lse


def temporal_back_body(ids, own, got, q, k, v, lse, w, g, dn_own, dn_send, dqkv, do):
    i = pl.program_id(0)
    b, r, d = g.shape
    f = own.shape[0]

    @pl.when(i == 0)
    def _():
        in_blocks(own, got, g)
        wo = weight(w, 3)
        step = b * r // 4
        for c in range(4):
            at = slice(c * step, (c + 1) * step)
            do[at] = nt(g[...].reshape(b * r, d)[at], wo).astype(BF)

    at = pl.ds(pl.multiple_of(i * r, r), r)
    attend_back(
        q, k, v, do.at[at], lse.at[0],
        dqkv.at[0, at], dqkv.at[1, at], dqkv.at[2, at], same_place(place_bias(r)),
    )

    @pl.when(i == pl.num_programs(0) - 1)
    def _():
        ws = [weight(w, c) for c in range(3)]
        acc = nn(dqkv[0], ws[0]) + nn(dqkv[1], ws[1]) + nn(dqkv[2], ws[2])
        for s in range(b):
            m = acc[s * r : (s + 1) * r].reshape(2 * f, 8, d).astype(BF)
            dn_own[:, s] = m[:f]
            dn_send[:, s] = m[f:]


def temporal_back(ids, own, got, q, k, v, lse, w):
    f, half, d = own.shape
    b, r = half // 8, 16 * f
    own, got = own.reshape(f, b, 8, d), got.reshape(f, b, 8, d)
    res = call(
        temporal_back_body, "temporal_back", 34, ids, (b,),
        [whole(own.shape), whole(got.shape)]
        + [pl.BlockSpec((r, d), lambda i, t: (i, 0))] * 3
        + [pl.BlockSpec((1, d // GROUP, PER * r), lambda i, t: (i, 0, 0)),
           whole((1,) + w.shape[1:], (1, 0, 0, 0, 0))],
        [whole((b, r, d)), whole(own.shape), whole(own.shape), whole((3, b * r, d))],
        [struct((b, r, d), BF), struct(own.shape, BF), struct(own.shape, BF),
         struct((3, b * r, d), BF)],
        (own, got, q, k, v, lse, w),
        [pltpu.VMEM((b * r, d), BF)],
    )
    g, dn_own, dn_send, dqkv = res
    return g, dn_own.reshape(f, half, d), dn_send.reshape(f, half, d), dqkv


def weight_grads_body(ids, dqkv, o_in, n, g_in, send, keep, sums, o, g, sem):
    c = pl.program_id(0)

    def loads():
        return [pltpu.make_async_copy(a, b, sem.at[z])
                for z, (a, b) in enumerate(((o_in, o), (g_in, g)))]

    @pl.when(c == 0)
    def _():
        for v in loads():
            v.start()

    d = n.shape[1]
    e = d // 4

    def put(m):
        m = m.astype(BF)
        for r in range(4):
            to = send if r % 2 else keep
            to[r // 2, 0] = m[r * e : (r + 1) * e]

    @pl.when(c < 3)
    def _():
        v = dqkv[0]
        put(tn(v, n[...]))
        sums[0] = jnp.sum(v.astype(F32), axis=0, keepdims=True)

    @pl.when(c == 3)
    def _():
        for v in loads():
            v.wait()
        put(tn(o[...], g[...]))
        sums[0] = jnp.zeros_like(sums[0])


def weight_grads(ids, dqkv, o, n, g):
    d = n.shape[-1]
    rows = n.size // d
    dqkv = dqkv.reshape(3, rows, d)
    o, n, g = (v.reshape(rows, d) for v in (o, n, g))
    out = pl.BlockSpec((2, 1, d // 4, d), lambda c, t: (0, c, 0, 0))
    return call(
        weight_grads_body, "weight_grads", 13, ids, (4,),
        [pl.BlockSpec((1, rows, d), lambda c, t: (jnp.minimum(c, 2), 0, 0))]
        + [ANY, whole((rows, d)), ANY],
        [out, out, pl.BlockSpec((1, 1, d), lambda c, t: (c, 0, 0))],
        [struct((2, 4, d // 4, d), BF)] * 2 + [struct((4, 1, d), F32)],
        (dqkv, o, n, g),
        [pltpu.VMEM((rows, d), BF), pltpu.VMEM((rows, d), BF), pltpu.SemaphoreType.DMA((2,))],
    )


def spatial_back_body(ids, x, s1, dn_own, dn_got, g2, q, k, v, lse, w, gain, shift, *refs):
    g0, sums, dqkv, n0, gb, rows, do = refs[-7:]
    i = pl.program_id(0)
    f, r, d = rows.shape
    places = x.shape[-2]

    @pl.when(i == 0)
    def _():
        sums[...] = jnp.zeros_like(sums)
        rows[...] = jnp.zeros_like(rows)

    def add(at, val):
        sums[at : at + 1] += jnp.sum(val, axis=0, keepdims=True)

    def three(m):
        return m.reshape(f, r, d)

    hat, inv = hat_of(s1[...].reshape(f * r, d))
    dn = joined(dn_own[...], dn_got[...]).reshape(f * r, d)
    add(2, dn * hat)
    add(3, dn)
    g1 = g2[...].reshape(f * r, d) + hat_back(hat, inv, gain[1:2], dn)
    add(4, g1)
    gv = g1.astype(BF)
    gb[...] = three(gv)
    do[...] = three(nt(gv, weight(w, 3)).astype(BF))
    for j in range(f):
        attend_back(
            q.at[j], k.at[j], v.at[j], do.at[j], lse.at[j],
            dqkv.at[0, j], dqkv.at[1, j], dqkv.at[2, j], only_places(places),
        )
    rows[:, :places] = x[...].reshape(f, places, d).astype(F32)
    hat, inv = hat_of(rows[...].reshape(f * r, d))
    n0[...] = three((hat * gain[0:1] + shift[0:1]).astype(BF))
    dn = nn(dqkv[0].reshape(f * r, d), weight(w, 0))
    dn += nn(dqkv[1].reshape(f * r, d), weight(w, 1))
    dn += nn(dqkv[2].reshape(f * r, d), weight(w, 2))
    add(0, dn * hat)
    add(1, dn)
    out = three(g1 + hat_back(hat, inv, gain[0:1], dn))
    g0[...] = out[:, : g0.shape[1]].astype(g0.dtype)


def spatial_back(ids, x, s1, dn_own, dn_got, g2, q, k, v, lse, w, gain, shift, near, before=()):
    frames, _, d = s1.shape
    places = x.shape[-2]
    steps = frames // 4
    begin = 0 if near else steps
    blk = pl.BlockSpec((2, ROWS, d), lambda i, t: (i + begin, 0, 0))
    part = pl.BlockSpec((2, HALF, d), lambda i, t: (i + begin, 0, 0))
    size = places if near else ROWS
    out = pl.BlockSpec((2, size, d), lambda i, t: (i, 0, 0))
    big = struct((frames, ROWS, d), BF)
    return call(
        spatial_back_body, "spatial_back", 20, ids, (steps,),
        [tokens_spec(near, places, d), blk, part, part] + [blk] * 4
        + [pl.BlockSpec((2, d // GROUP, PER * ROWS), lambda i, t: (i + begin, 0, 0)),
           whole((1,) + w.shape[1:]), whole(gain.shape), whole(shift.shape)] + [ANY] * len(before),
        [out, whole((8, d)),
         pl.BlockSpec((3, 2, ROWS, d), lambda i, t: (0, i + begin, 0, 0)), blk, blk],
        [struct((frames // 2, size, d), F32 if near else BF), struct((8, d), F32),
         struct((3, frames, ROWS, d), BF), big, big],
        (x, s1, dn_own, dn_got, g2, q, k, v, lse, w, gain, shift) + tuple(before),
        [pltpu.VMEM((2, ROWS, d), F32), pltpu.VMEM((2, ROWS, d), BF)],
        {13 + i: 2 + i for i in range(len(before))},
    )


def gelu_parts(u):
    cdf = 0.5 + 0.5 * lax.erf(u * 0.7071067811865476)
    return u * cdf, cdf + u * (jnp.exp(-0.5 * u * u) * 0.3989422804014327)


def mlp_load(parts, wt, wd, sem):
    a, b, ct, cd = parts
    x = lax.rem(lax.axis_index("dp"), 2)
    h = a.shape[0] // 2
    mine = pl.ds(pl.multiple_of(x * h, h), h)
    other = pl.ds(pl.multiple_of((1 - x) * h, h), h)
    copies = []
    for z, (w, c) in enumerate(((wt, ct), (wd, cd))):
        rows = pl.ds(z * h, h)
        copies.append(pltpu.make_async_copy(a.at[rows], w.at[0, mine], sem.at[3 * z]))
        copies.append(pltpu.make_async_copy(b.at[rows], w.at[0, other], sem.at[3 * z + 1]))
        copies.append(pltpu.make_async_copy(c, w.at[1], sem.at[3 * z + 2]))
    return copies


def mlp_tile(n2, gb, wt, wd, b, h_s, dr_s):
    u = nt(n2, wt) + b
    dh = nt(gb, wd)
    h, slope = gelu_parts(u)
    h = h.astype(BF)
    h_s[...] = h
    dr = (dh * slope).astype(BF)
    dr_s[...] = dr
    return nn(h, wd), nn(dr, wt)


def mlp_grads(s, n2, gb, h, dr, gwt, gwd, gbi):
    gwt[s] = tn(dr, n2).astype(BF)
    gwd[s] = tn(h, gb).astype(BF)
    gbi[s] = jnp.sum(dr.astype(F32), axis=0, keepdims=True)


def mlp_first_body(ids, s1, o_own, o_got, near, far, w, b, bout, gain, shift, *refs):
    parts = refs[:4]
    (s2, n2, gb, branch, dn, gwt, gwd, gbi,
     n2s, gbs, hs, drs, brs, dns, wt, wd, sem) = refs[4:]
    s, i = pl.program_id(0), pl.program_id(1)
    tile, d = n2.shape
    steps = n2s.shape[0]

    @pl.when((i == 0) & (s == 0))
    def _():
        for c in mlp_load(parts, wt, wd, sem):
            c.start()

    @pl.when(s == 0)
    def _():
        @pl.when(i < steps // 2)
        def _():
            gb[...] = near[...].reshape(tile, d)

        @pl.when(i >= steps // 2)
        def _():
            gb[...] = far[...].reshape(tile, d)

        f, n, _ = o_own.shape

        def flat(v):
            return v[...].astype(F32).reshape(f * n, d).astype(BF)

        wo = w[0, 3]
        turned = jnp.concatenate([wo[r] for r in (1, 0, 3, 2)])
        own = nn(flat(o_own), wo.reshape(d, d)).reshape(f, n, d)
        got = nn(flat(o_got), turned).reshape(f, n, d)
        v = s1[...] + (joined(own, got).reshape(s1.shape) + bout[1:2])
        s2[...] = v
        n = (hat_of(v)[0] * gain[2:3] + shift[2:3]).astype(BF)
        n2[...] = n
        n2s[i] = n
        gbs[i] = gb[...]

    @pl.when((i == 0) & (s == 0))
    def _():
        for c in mlp_load(parts, wt, wd, sem):
            c.wait()

    br, dv = mlp_tile(
        n2s[i], gbs[i], wt[s], wd[s], b[3 - 2 * s, 1:2], hs.at[i], drs.at[i]
    )

    @pl.when(s == 0)
    def _():
        brs[i] = br
        dns[i] = dv

    @pl.when(s == 1)
    def _():
        branch[...] = brs[i] + br
        dn[...] = dns[i] + dv

    @pl.when(i == steps - 1)
    def _():
        rows = steps * tile
        mlp_grads(s, *(v[...].reshape(rows, d) for v in (n2s, gbs, hs, drs)), gwt, gwd, gbi)


def mlp_scratch(steps, tile, d, h):
    return [pltpu.VMEM((steps, tile, d), BF), pltpu.VMEM((steps, tile, d), BF),
            pltpu.VMEM((steps, tile, h), BF), pltpu.VMEM((steps, tile, h), BF),
            pltpu.VMEM((steps, tile, d), F32), pltpu.VMEM((steps, tile, d), F32),
            pltpu.VMEM((2, h, d), BF), pltpu.VMEM((2, h, d), BF), pltpu.SemaphoreType.DMA((6,))]


def mlp_first(ids, s1, o_own, o_got, cot, far, w, b, bout, gain, shift, parts):
    frames, _, d = s1.shape
    tile = 2 * ROWS
    steps = frames // 2
    half = steps // 2
    rows = frames * ROWS
    h = parts[2].shape[0]

    def early(s, i):
        return jnp.where(s == 0, i, steps - 1)

    blk = pl.BlockSpec((tile, d), lambda s, i, t: (early(s, i), 0))
    part = pl.BlockSpec((2, HALF, d), lambda s, i, t: (early(s, i), 0, 0))
    late = pl.BlockSpec((tile, d), lambda s, i, t: (jnp.where(s == 0, 0, i), 0))
    return call(
        mlp_first_body, "mlp_first", 33, ids, (2, steps),
        [blk, part, part,
         pl.BlockSpec((2, ROWS, d), lambda s, i, t: (jnp.minimum(early(s, i), half - 1), 0, 0)),
         pl.BlockSpec((2, ROWS, d), lambda s, i, t: (jnp.maximum(early(s, i) - half, 0), 0, 0)),
         whole((1, 4) + w.shape[2:], (1, 0, 0, 0, 0)), whole(b.shape), whole(bout.shape),
         whole(gain.shape), whole(shift.shape)] + [ANY] * 4,
        [blk] * 3 + [late] * 2 + [whole((2, h, d)), whole((2, h, d)), whole((2, 1, h))],
        [struct((rows, d), F32), struct((rows, d), BF), struct((rows, d), BF),
         struct((rows, d), F32), struct((rows, d), F32), struct((2, h, d), BF),
         struct((2, h, d), BF), struct((2, 1, h), F32)],
        (s1.reshape(rows, d), o_own, o_got, cot, far, w, b, bout, gain, shift) + tuple(parts),
        mlp_scratch(steps, tile, d, h),
    )


def mlp_second_body(ids, s2, n2, gb, br0, dn0, b, bdown, gain, *refs):
    parts = refs[:4]
    (near, far, g2, g_own, g_send, gwt, gwd, gbi, sums,
     n2s, gbs, hs, drs, brs, dns, wt, wd, sem) = refs[4:]
    s, i = pl.program_id(0), pl.program_id(1)
    tile, d = n2.shape
    steps = n2s.shape[0]

    @pl.when((i == 0) & (s == 0))
    def _():
        sums[...] = jnp.zeros_like(sums)
        for c in mlp_load(parts, wt, wd, sem):
            c.start()

    @pl.when(s == 0)
    def _():
        n2s[i] = n2[...]
        gbs[i] = gb[...]

    @pl.when((i == 0) & (s == 0))
    def _():
        for c in mlp_load(parts, wt, wd, sem):
            c.wait()

    br, dv = mlp_tile(
        n2s[i], gbs[i], wt[s], wd[s], b[2 - 2 * s, 1:2], hs.at[i], drs.at[i]
    )

    @pl.when(s == 0)
    def _():
        brs[i] = br0[...] + br
        dns[i] = dn0[...] + dv

    @pl.when(i == steps - 1)
    def _():
        rows = steps * tile
        mlp_grads(s, *(v[...].reshape(rows, d) for v in (n2s, gbs, hs, drs)), gwt, gwd, gbi)

    @pl.when(s == 1)
    def _():
        def add(at, val):
            sums[at : at + 1] += jnp.sum(val, axis=0, keepdims=True)

        v = s2[...]
        f, places, _ = near.shape
        out = (v + (brs[i] + br + bdown[...])).reshape(f, ROWS, d)

        @pl.when(i < steps // 2)
        def _():
            near[...] = out[:, :places]

        @pl.when(i >= steps // 2)
        def _():
            far[...] = out.astype(BF)

        hat, inv = hat_of(v)
        dt = dns[i] + dv
        add(0, dt * hat)
        add(1, dt)
        g3 = gbs[i].astype(F32)
        add(3, g3)
        g = g3 + hat_back(hat, inv, gain[2:3], dt)
        add(2, g)
        g = g.reshape(f, ROWS, d)
        g2[...] = g
        parted(g, g_own, g_send)


def mlp_second(ids, s2, n2, gb, br0, dn0, b, bdown, gain, parts, shape):
    rows, d = s2.shape
    _, n, places, _ = shape
    frames = rows // ROWS
    steps = frames // 2
    half = steps // 2
    tile = 2 * ROWS
    h = parts[2].shape[0]

    def late(s, i):
        return jnp.where(s == 0, 0, i)

    blk = pl.BlockSpec((tile, d), lambda s, i, t: (jnp.where(s == 0, i, steps - 1), 0))
    end = pl.BlockSpec((tile, d), lambda s, i, t: (late(s, i), 0))
    three = pl.BlockSpec((2, ROWS, d), lambda s, i, t: (late(s, i), 0, 0))
    part = pl.BlockSpec((2, HALF, d), lambda s, i, t: (late(s, i), 0, 0))
    return call(
        mlp_second_body, "mlp_second", 33, ids, (2, steps),
        [end] + [blk] * 4 + [whole(b.shape), whole(bdown.shape), whole(gain.shape)] + [ANY] * 4,
        [pl.BlockSpec((2, places, d), lambda s, i, t: (jnp.minimum(late(s, i), half - 1), 0, 0)),
         pl.BlockSpec((2, ROWS, d), lambda s, i, t: (jnp.maximum(late(s, i) - half, 0), 0, 0)),
         three, part, part, whole((2, h, d)), whole((2, h, d)), whole((2, 1, h)), whole((8, d))],
        [struct((n, places, d), F32), struct((n, ROWS, d), BF), struct((frames, ROWS, d), F32),
         struct((frames, HALF, d), BF), struct((frames, HALF, d), BF), struct((2, h, d), BF),
         struct((2, h, d), BF), struct((2, 1, h), F32), struct((8, d), F32)],
        (s2, n2, gb, br0, dn0, b, bdown, gain) + tuple(parts),
        mlp_scratch(steps, tile, d, h),
    )


def both_clips_body(ids, near, got, out):
    mine = pl.program_id(0) == ids[0]
    f, places, _ = near.shape

    @pl.when(mine)
    def _():
        for j in range(f):
            out[0, :, j] = near[j]

    @pl.when(jnp.logical_not(mine))
    def _():
        for j in range(f):
            out[0, :, j] = got[j, :places].astype(F32)


def both_clips(ids, near, got):
    n, places, d = near.shape
    out = call(
        both_clips_body, "both_clips", 6, ids, (2,),
        [whole(near.shape), whole(got.shape)],
        pl.BlockSpec((1, places, n, d), lambda i, t: (i, 0, 0, 0)),
        struct((2, places, n, d), F32),
        (near, got),
    )
    return out.transpose(0, 2, 1, 3)


def shape_body(ids, f0, f1, m, mo, gqkv, gout, gwin, gwd):
    x = lax.rem(lax.axis_index("dp"), 2)
    for i, f in enumerate((f0, f1)):
        for c in range(3):
            gqkv[i, c] = f[c].astype(F32)
        gout[i] = f[3].astype(F32)
    n = m.shape[0] // 2
    lo = jnp.where(x == 0, m[...], mo[...]).astype(F32)
    hi = jnp.where(x == 0, mo[...], m[...]).astype(F32)
    gwin[:, :n] = lo[:n].T
    gwin[:, n:] = hi[:n].T
    gwd[:n] = lo[n:]
    gwd[n:] = hi[n:]


def to_results(ids, f0, f1, m, mo):
    _, e, d = f0.shape
    h = m.shape[0]
    shapes = [(2, 3, e, d), (2, e, d), (d, h), (h, d)]
    return call(
        shape_body, "to_results", 5, ids, (1,),
        [whole(v.shape) for v in (f0, f1, m, mo)],
        [whole(v) for v in shapes],
        [struct(v, F32) for v in shapes],
        (f0, f1, m, mo),
    )


def finish_body(dp, t0, t1, rel, rep, f0, f1, rel_o, rep_o, *scratch):
    (tt, zr, ta, tb, aa, ab, xs, rel_r, rep_r, rel_s, rep_s, send, recv) = scratch
    me_d, me_t = lax.axis_index("dp"), lax.axis_index("tensor")
    x = lax.rem(me_d, 2)
    bits = []
    bit = 2
    while bit < dp:
        bits.append(bit)
        bit *= 2

    def flip(v, b):
        return v + b - 2 * b * lax.rem(v // b, 2)

    def core():
        return (me_d, flip(me_t, 1))

    def over_y():
        return (me_d, flip(me_t, 2))

    def over_d(b):
        return (flip(me_d, b), me_t)

    partners = [core(), over_y(), over_d(1)] + [over_d(b) for b in bits]
    barrier = pltpu.get_barrier_semaphore()
    for p in partners:
        pl.semaphore_signal(barrier, inc=1, device_id=p, device_id_type=pl.DeviceIdType.MESH)
    pl.semaphore_wait(barrier, len(partners))

    count = [0]

    def copy(src, dst, to):
        k = count[0]
        count[0] += 1
        c = pltpu.make_async_remote_copy(
            src_ref=src, dst_ref=dst, send_sem=send.at[k], recv_sem=recv.at[k],
            device_id=to, device_id_type=pl.DeviceIdType.MESH,
        )
        c.start()
        return c

    def plus(a, b):
        return (a.astype(F32) + b.astype(F32)).astype(BF)

    n = tt.shape[1]

    def rest(k, out):
        size, held = n, tt.at[k]
        done = []
        for z, b in enumerate(bits[:2]):
            half = size // 2
            bitv = lax.rem(me_d // b, 2)
            mine = pl.multiple_of(bitv * half, 16)
            other = pl.multiple_of((1 - bitv) * half, 16)
            dst = zr.at[k, z, pl.ds(0, half)]
            c = copy(held.at[pl.ds(other, half)], dst, over_d(b))
            yield
            c.wait()
            nxt = (ta if z == 0 else tb).at[k]
            nxt[...] = plus(held[pl.ds(mine, half)], dst[...])
            done.append(((aa if z == 0 else ab).at[k], mine, half, b))
            size, held = half, nxt
        for z, b in enumerate(bits[2:]):
            dst = zr.at[k, 2 + z, pl.ds(0, size)]
            c = copy(held, dst, over_d(b))
            yield
            c.wait()
            held[...] = plus(held[...], dst[...])
        for z, (up, mine, half, b) in enumerate(reversed(done)):
            up[pl.ds(mine, half)] = held[...]
            c = copy(up.at[pl.ds(mine, half)], up.at[pl.ds(mine, half)], over_d(b))
            yield
            c.wait()
            held = up
        c = copy(held, xs.at[k, 0], over_d(1))
        yield
        c.wait()
        out(held, xs.at[k, 0])

    def attn0(j):
        tt[j] = t0[j]

        def out(mine, got):
            f0[j + 2 * x] = mine[...]
            f0[j + 2 * (1 - x)] = got[...]

        yield from rest(j, out)

    def attn1():
        c = copy(t1, xs.at[2], over_d(1))
        f1[pl.ds(2 * x, 2)] = t1[...]
        yield
        yield
        yield
        c.wait()
        f1[pl.ds(2 - 2 * x, 2)] = xs[2]

    def small():
        rel_s[...] = rel[...]
        rep_s[...] = rep[...]
        for z, (to, b) in enumerate([(core(), 1), (over_y(), 2)]):
            c = [copy(rel_s, rel_r.at[z], to), copy(rep_s, rep_r.at[z], to)]
            yield
            for v in c:
                v.wait()
            rep_s[...] += rep_r[z]
            for r in range(4):
                rel_s[r] = rel_s[r] + rel_r[z, r ^ b]
        for z, b in enumerate([1] + bits):
            c = [
                copy(rel_s.at[0], rel_r.at[2 + z, 0], over_d(b)),
                copy(rep_s, rep_r.at[2 + z], over_d(b)),
            ]
            yield
            for v in c:
                v.wait()
            rep_s[...] += rep_r[2 + z]
            rel_s[0] = rel_s[0] + rel_r[2 + z, 0]
        rel_o[...] = rel_s[0]
        rep_o[...] = rep_s[...]

    chains = [attn0(0), attn0(1), attn1(), small()]
    while chains:
        left = []
        for chain in chains:
            try:
                next(chain)
                left.append(chain)
            except StopIteration:
                pass
        chains = left


def finish(t0, t1, rel, rep, dp):
    _, n, d = t0.shape
    nb = max(dp.bit_length() - 2, 0)
    vm = pl.BlockSpec(memory_space=pltpu.VMEM)
    return pl.pallas_call(
        functools.partial(finish_body, dp),
        in_specs=[vm] * 4,
        out_specs=[vm] * 4,
        out_shape=[struct((4, n, d), BF)] * 2 + [struct(rel.shape[1:], F32), struct(rep.shape, F32)],
        scratch_shapes=[
            pltpu.VMEM((2, n, d), BF),
            pltpu.VMEM((2, max(nb, 1), n // 2, d), BF),
            pltpu.VMEM((2, n // 2, d), BF),
            pltpu.VMEM((2, n // 4, d), BF),
            pltpu.VMEM((2, n, d), BF),
            pltpu.VMEM((2, n // 2, d), BF),
            pltpu.VMEM((3, 2, n, d), BF),
            pltpu.VMEM((3 + nb,) + rel.shape, F32),
            pltpu.VMEM((3 + nb,) + rep.shape, F32),
            pltpu.VMEM(rel.shape, F32),
            pltpu.VMEM(rep.shape, F32),
            pltpu.SemaphoreType.DMA((96,)),
            pltpu.SemaphoreType.DMA((96,)),
        ],
        compiler_params=pltpu.CompilerParams(
            collective_id=0, has_side_effects=True, vmem_limit_bytes=LIMIT
        ),
        name="finish",
        cost_estimate=cost(40),
    )(t0, t1, rel, rep)


def shards(clips, cot, gain, shift, qkv, qvb, wout, bout, win, b_in, wdown, bdown):
    tensor = lax.axis_index("tensor")
    y = tensor // 2
    x = lax.axis_index("dp") % 2
    dp = lax.axis_size("dp")
    width = clips.shape[-1]
    e = qkv.shape[-1]
    h = win.shape[1] // 2
    ids = y.reshape(1).astype(jnp.int32)

    def over_tensor(v, bit):
        return lax.ppermute(v, "tensor", [(i, i ^ bit) for i in range(4)])

    def over_dp(v, bit):
        return lax.ppermute(v, "dp", [(i, i ^ bit) for i in range(dp)])

    def after(v, *others):
        return lax.optimization_barrier((v,) + others)[0]

    def pick(v, axis):
        n = v.shape[axis] // 2
        return (
            lax.dynamic_slice_in_dim(v, x * n, n, axis),
            lax.dynamic_slice_in_dim(v, (1 - x) * n, n, axis),
        )

    def padded(v):
        return jnp.pad(v, ((0, 0), (0, ROWS - v.shape[1]), (0, 0)))

    bias = jnp.concatenate([qvb.reshape(1, -1), b_in.reshape(1, -1), jnp.zeros((6, width), F32)])
    w, clips_far, b = start(qkv.transpose(0, 1, 3, 2), wout, bias, clips)
    win_t = win.T
    z = lax.axis_index("dp") // 2 % 2
    n = h // 2
    at = x * h + z * n
    sent = [jnp.concatenate([lax.dynamic_slice_in_dim(v, at, n, 0) for v in (win_t, wdown)])]
    sent.append(padded(lax.dynamic_index_in_dim(cot, 1 - y, 0, False)))
    w, *sent = lax.optimization_barrier((w, *sent))
    m_q = over_tensor(sent[0], 2)
    cot_far = over_tensor(sent[1], 2)
    m_c = [over_tensor(after(v, w), 1) for v in (win_t, wdown)]
    qv = b[:, 0].reshape(4, 4, e).transpose(1, 0, 2).reshape(4, width)

    some = spatial(ids, clips, w, gain, shift, qv, bout, True)
    clips_far, m_q = lax.optimization_barrier((clips_far, m_q))
    m_z = over_dp(m_q, 2)
    s1, n_own, n_send, q0, k0, v0, o0, lse0 = spatial(
        ids, clips_far, w, gain, shift, qv, bout, False, some
    )
    n_own, m_z = lax.optimization_barrier((n_own, m_z))
    m_a, m_b = jnp.where(z == 0, m_q, m_z), jnp.where(z == 0, m_z, m_q)
    m_y = jnp.concatenate([m_a[:n], m_b[:n], m_a[n:], m_b[n:]])
    m_x = over_dp(m_y, 1)
    m_cy = over_tensor(m_y, 1)
    n1p, q1, k1, v1, o1p, o_own, o_send, lse1 = temporal(
        ids, n_own, over_tensor(n_send, 1), w, qv
    )
    m_cx = over_tensor(m_x, 1)
    cot_near = padded(lax.dynamic_index_in_dim(after(cot, w), y, 0, False))

    first = (m_cy, m_cx, m_c[0], m_c[1])
    second = (m_y, m_x, win_t, wdown)
    s2, n2, gb3, branch, dn2, gwt_a, gwd_a, gb_a = mlp_first(
        ids, s1, o_own, over_tensor(o_send, 1), cot_near, cot_far, w, b, bout, gain, shift, first
    )
    out_near, far, g2, g_own, g_send, gwt_b, gwd_b, gb_b, sums2 = mlp_second(
        ids, s2, n2, gb3, branch, dn2, b, bdown[None], gain, second, clips.shape
    )

    g_got = over_tensor(g_send, 1)
    keep_t = gwt_b + over_tensor(gwt_a, 1)
    keep_d = gwd_b + over_tensor(gwd_a, 1)
    g_got, keep_t, keep_d = lax.optimization_barrier((g_got, keep_t, keep_d))
    got_t = over_tensor(keep_t[0], 2)
    mine_d, send_d = pick(keep_d, 1)
    got_d = over_dp(send_d, 1)
    out_got = over_tensor(after(far, got_t), 2)

    g2p, dn_own, dn_send, dqkv1 = temporal_back(ids, g_own, g_got, q1, k1, v1, lse1, w)
    dn_got = over_tensor(dn_send, 1)
    mine_t, send_t = pick(keep_t[1] + got_t, 0)
    mine_d = mine_d + got_d
    g2p, mine_t, send_t, mine_d = lax.optimization_barrier((g2p, mine_t, send_t, mine_d))
    got_t = over_dp(send_t, 1)
    got_d = over_tensor(mine_d[0], 2)
    gs1, gk1, sums1 = weight_grads(ids, dqkv1, o1p, n1p, g2p)
    mlp_sum = jnp.concatenate([mine_t + got_t, mine_d[1] + got_d])
    dn_got, gs1, mlp_sum = lax.optimization_barrier((dn_got, gs1, mlp_sum))
    groups = [[i for i in range(dp) if i % 2 == p] for p in range(2)]
    if dp > 2:
        mlp_sum = lax.psum(mlp_sum, "dp", axis_index_groups=groups)
    got1 = over_tensor(gs1, 1)
    kept = (s1, dn_own, dn_got, g2, q0, k0, v0, lse0, w, gain, shift)
    g0_far, sums_f, *rest = spatial_back(ids, clips_far, *kept, False)
    mine1, send1 = pick(gk1 + got1, 1)
    rest[0], mine1, send1, out_got = lax.optimization_barrier((rest[0], mine1, send1, out_got))
    got_x = over_dp(send1[0], 1)
    got_y = over_tensor(mine1[1], 2)
    got_xy = lax.ppermute(
        send1[1], ("dp", "tensor"), [(i, ((i // 4) ^ 1) * 4 + (i % 4 ^ 2)) for i in range(4 * dp)]
    )
    grad_near, sums_n, dqkv0, n0, gb0 = spatial_back(ids, clips, *kept, True, rest)
    t1 = (mine1[0] + got_x) + (got_y + got_xy)
    gb0, t1, mlp_sum = lax.optimization_barrier((gb0, t1, mlp_sum))
    gs0, gk0, sums_b = weight_grads(ids, dqkv0, o0, n0, gb0)

    bits = [1 << k for k in range(1, dp.bit_length() - 1)]
    z1 = over_dp(t1, bits[0]) if bits else jnp.zeros_like(t1)
    gs0, gk0, z1 = lax.optimization_barrier((gs0, gk0, z1))
    t1 = t1 + z1
    for bit in bits[1:]:
        t1 = t1 + over_dp(t1, bit)
    got0 = over_tensor(gs0, 1)
    output = both_clips(ids, out_near, after(out_got, gs0))
    keep0 = (gk0 + got0).reshape(2, 2, 2, e, width)
    mine0, send0 = (v[:, 0] for v in pick(keep0, 1))
    got_y = over_tensor(jnp.stack([mine0[1, 0], send0[1, 0]]), 2)
    got_x = over_dp(send0[:, 1], 1)
    mlp_got = over_dp(mlp_sum, 1)
    output, got_y, got_x, t1 = lax.optimization_barrier((output, got_y, got_x, t1))
    in_got = over_tensor(after(g0_far, got_y), 2)
    got_a = over_dp(send0[0, 0] + got_y[1], 1)
    got_b = over_tensor(mine0[1, 1] + got_x[1], 2)
    t0 = jnp.stack([mine0[0, 0] + got_y[0] + got_a, mine0[0, 1] + got_x[0] + got_b])
    sums0 = sums_f + sums_n
    rep = jnp.stack(
        [sums0[0], sums0[2], sums2[0], sums0[1], sums0[3], sums2[1], sums0[4], sums2[2], sums2[3]]
    )
    rep = jnp.pad(rep, ((0, 7), (0, 0)))
    qvs = jnp.stack([sums_b[0, 0], sums_b[2, 0], sums1[0, 0], sums1[2, 0]])
    qvs = qvs.reshape(4, 4, e).transpose(1, 0, 2).reshape(4, 1, 4 * e)
    hid = jnp.stack([gb_b[1], gb_a[1], gb_b[0], gb_a[0]])
    rel = jnp.concatenate([qvs, hid, jnp.zeros((4, 6, width), F32)], axis=1)
    f0, f1, rel, rep = finish(t0, t1, rel, rep, dp)
    input_grad = both_clips(ids, grad_near, after(in_got, f0))
    gqkv, gout, gwin, gwd = to_results(ids, f0, f1, mlp_sum, mlp_got)
    gqkv = gqkv.transpose(0, 1, 3, 2)
    return (
        output,
        input_grad,
        rep[0:3],
        rep[3:6],
        gqkv,
        rel[0].reshape(2, 2, e),
        gout,
        rep[6:8],
        gwin,
        rel[1],
        gwd,
        rep[8],
    )


def solution(mesh):
    placed = (
        P("dp", "tensor", None, None),
        P("dp", "tensor", None, None),
        P(),
        P(),
        P(None, None, None, "tensor"),
        P(None, None, "tensor"),
        P(None, "tensor", None),
        P(),
        P(None, "tensor"),
        P("tensor"),
        P("tensor", None),
        P(),
    )
    return jax.shard_map(
        shards,
        mesh=mesh,
        in_specs=placed,
        out_specs=(
            P("dp", "tensor", None, None),
            P("dp", "tensor", None, None),
            P(),
            P(),
            P(None, None, None, "tensor"),
            P(None, None, "tensor"),
            P(None, "tensor", None),
            P(),
            P(None, "tensor"),
            P("tensor"),
            P("tensor", None),
            P(),
        ),
        check_vma=False,
    )
```

```python
import functools

import jax
import jax.numpy as jnp
from jax import lax
from jax.experimental import pallas as pl
from jax.experimental.pallas import tpu as pltpu
from jax.sharding import PartitionSpec as P

BF = jnp.bfloat16
F32 = jnp.float32
HEAD_DIM = 64
norm_epsilon = 1e-06
LIMIT = 60 << 20
ROWS = 208
HALF = ROWS // 2


def nn(a, b):
    return lax.dot_general(a, b, (((1,), (0,)), ((), ())), preferred_element_type=F32)


def nt(a, b):
    return lax.dot_general(a, b, (((1,), (1,)), ((), ())), preferred_element_type=F32)


def tn(a, b):
    return lax.dot_general(a, b, (((0,), (0,)), ((), ())), preferred_element_type=F32)


def hat_of(values):
    mean = jnp.mean(values, axis=-1, keepdims=True)
    centered = values - mean
    inv = lax.rsqrt(jnp.mean(centered * centered, axis=-1, keepdims=True) + norm_epsilon)
    return centered * inv, inv


def hat_back(hat, inv, gain, grad):
    e = grad * gain
    return inv * (
        e - jnp.mean(e, axis=-1, keepdims=True) - hat * jnp.mean(e * hat, axis=-1, keepdims=True)
    )


GROUP = 256
PER = GROUP // HEAD_DIM


def head_of_lane(rows):
    return lax.broadcasted_iota(jnp.int32, (rows, GROUP), 1) // HEAD_DIM


def stacked(v):
    lane = head_of_lane(v.shape[0])
    return jnp.concatenate([jnp.where(lane == h, v, jnp.zeros_like(v)) for h in range(PER)])


def unstacked(v):
    rows = v.shape[0] // PER
    lane = head_of_lane(rows)
    out = v[:rows]
    for h in range(1, PER):
        out = jnp.where(lane == h, v[h * rows : (h + 1) * rows], out)
    return out


def only_places(places):
    def mask(s):
        cut = places // 8 * 8
        row = lax.broadcasted_iota(jnp.int32, (s.shape[0] - cut, s.shape[1]), 0)
        return jnp.concatenate([s[:cut], jnp.where(row < places - cut, s[cut:], -1e30)])

    return mask


def same_place(bias):
    return lambda s: s + bias


def place_bias(rows):
    a = lax.broadcasted_iota(jnp.int32, (rows, PER * rows), 0) & 7
    b = lax.broadcasted_iota(jnp.int32, (rows, PER * rows), 1) & 7
    return jnp.where(a == b, 0.0, -1e30).astype(F32)


def attend(q, k, v, o, lse, mask):
    spans = [slice(a, a + GROUP) for a in range(0, q.shape[1], GROUP)]
    s = [mask(nt(k[:, at], stacked(q[:, at]))) for at in spans]
    top = [jnp.max(m, axis=0, keepdims=True) for m in s]
    ex = [jnp.exp(m - t) for m, t in zip(s, top)]
    total = [jnp.sum(m, axis=0, keepdims=True) for m in ex]
    p = [(m * (1.0 / t)).astype(BF) for m, t in zip(ex, total)]
    r = [tn(m, v[:, at]) for m, at in zip(p, spans)]
    for g, at in enumerate(spans):
        o(at, unstacked(r[g]))
        lse[g : g + 1] = top[g] + jnp.log(total[g])


def attend_back(q, k, v, do, lse, dq, dk, dv, mask):
    spans = [slice(a, a + GROUP) for a in range(0, q.shape[1], GROUP)]
    qs = [stacked(q[:, at]) for at in spans]
    dos = [stacked(do[:, at]) for at in spans]
    s = [mask(nt(k[:, at], m)) for at, m in zip(spans, qs)]
    dp = [nt(v[:, at], m) for at, m in zip(spans, dos)]
    p = [jnp.exp(m - lse[g : g + 1]) for g, m in enumerate(s)]
    row = [jnp.sum(a * b, axis=0, keepdims=True) for a, b in zip(p, dp)]
    ds = [(a * (b - t)).astype(BF) for a, b, t in zip(p, dp, row)]
    for g, at in enumerate(spans):
        dv[:, at] = nn(p[g].astype(BF), dos[g]).astype(BF)
        dk[:, at] = nn(ds[g], qs[g]).astype(BF)
    r = [tn(m, k[:, at]) for m, at in zip(ds, spans)]
    for g, at in enumerate(spans):
        dq[:, at] = (unstacked(r[g]) * HEAD_DIM**-0.5).astype(BF)


def whole(shape, index=None):
    index = (0,) * len(shape) if index is None else index
    return pl.BlockSpec(shape, lambda *_: index, pipeline_mode=pl.Buffered(1))


def cost(us):
    return pl.CostEstimate(flops=int(us * 1.1e9), bytes_accessed=int(us * 1e5), transcendentals=0)


def struct(shape, kind):
    return jax.ShapeDtypeStruct(shape, kind)


ANY = pl.BlockSpec(memory_space=pl.ANY)
MESH = pl.DeviceIdType.MESH


def call(body, name, us, ids, grid, in_specs, out_specs, out_shape, args, scratch=(), aliases=None):
    return pl.pallas_call(
        body,
        grid_spec=pltpu.PrefetchScalarGridSpec(
            num_scalar_prefetch=1,
            grid=grid,
            in_specs=in_specs,
            out_specs=out_specs,
            scratch_shapes=list(scratch),
        ),
        out_shape=out_shape,
        input_output_aliases=aliases or {},
        compiler_params=pltpu.CompilerParams(
            dimension_semantics=("arbitrary",) * len(grid), vmem_limit_bytes=LIMIT
        ),
        name=name,
        cost_estimate=cost(us),
    )(ids, *args)


def core_index():
    return lax.rem(lax.axis_index("tensor"), 2)


def joined(own, got):
    first = core_index() == 0
    a, b = own.astype(F32), got.astype(F32)
    return jnp.concatenate([jnp.where(first, a, b), jnp.where(first, b, a)], axis=-2)


def parted(v, own, send):
    first = core_index() == 0
    n = v.shape[1] // 2
    a, b = v[:, :n], v[:, n:]
    own[...] = jnp.where(first, a, b).astype(BF)
    send[...] = jnp.where(first, b, a).astype(BF)


def in_blocks(own, got, out):
    f, blocks, _, d = own.shape
    for b in range(blocks):
        both = [v[:, b].astype(F32).reshape(f * 8, d) for v in (own, got)]
        out[b] = jnp.concatenate(both).astype(BF)


def start_body(qkv, wout, bias, clips, w, far, b, own, send, recv, local):
    me_d, me_t = lax.axis_index("dp"), lax.axis_index("tensor")
    x, y = lax.rem(me_d, 2), me_t // 2
    core = (me_d, me_t + 1 - 2 * lax.rem(me_t, 2))
    over_y = (me_d, me_t + 2 - 4 * y)
    over_x = (me_d + 1 - 2 * x, me_t)
    z = lax.rem(me_d // 2, 2)
    over_z = (me_d + 2 - 4 * z, me_t)
    loads = []
    for i in range(2):
        loads.append(pltpu.make_async_copy(qkv.at[i], own.at[i, 0:3], local.at[3 * i]))
        loads.append(pltpu.make_async_copy(wout.at[i], own.at[i, 3], local.at[3 * i + 1]))
    for c in loads:
        c.start()
    barrier = pltpu.get_barrier_semaphore()
    for to in (core, over_y, over_x, over_z):
        pl.semaphore_signal(barrier, inc=1, device_id=to, device_id_type=MESH)
    pl.semaphore_wait(barrier, 4)
    count = [0]

    def copy(src, dst, to):
        k = count[0]
        count[0] += 1
        c = pltpu.make_async_remote_copy(
            src_ref=src, dst_ref=dst, send_sem=send.at[k], recv_sem=recv.at[k],
            device_id=to, device_id_type=MESH,
        )
        c.start()
        return c

    one, two = 2 * x + z, 2 * x + 1 - z
    mine, other = pl.ds(2 * x, 2), pl.ds(2 - 2 * x, 2)
    done, ys, zs, xs = [], [], [], []
    for i in range(2):
        loads[2 * i].wait()
        loads[2 * i + 1].wait()
        ys.append(copy(own.at[i, one], w.at[i, one, 2], over_y))
    done.append(copy(clips.at[1 - y], far, over_y))
    for i in range(2):
        done.append(copy(own.at[i], w.at[i, :, 1], core))
        c = pltpu.make_async_copy(own.at[i], w.at[i, :, 0], local.at[3 * i + 2])
        c.start()
        done.append(c)
    b[0] = bias[...]
    done.append(copy(b.at[0], b.at[1], core))
    by = copy(b.at[0], b.at[2], over_y)
    for i in range(2):
        ys[i].wait()
        zs.append(copy(w.at[i, one, 2], w.at[i, one, 2], over_z))
        done.append(copy(w.at[i, one, 2], w.at[i, one, 3], core))
    for i in range(2):
        zs[i].wait()
        xs.append(copy(w.at[i, mine, 2], w.at[i, mine, 2], over_x))
        done.append(copy(w.at[i, two, 2], w.at[i, two, 3], core))
    for i in range(2):
        xs[i].wait()
        done.append(copy(w.at[i, other, 2], w.at[i, other, 3], core))
    by.wait()
    done.append(copy(b.at[2], b.at[3], core))
    for c in done:
        c.wait()


def start(qkv, wout, bias, clips):
    _, _, e, d = qkv.shape
    return pl.pallas_call(
        start_body,
        in_specs=[ANY, ANY, pl.BlockSpec(memory_space=pltpu.VMEM), ANY],
        out_specs=[ANY, ANY, pl.BlockSpec(memory_space=pltpu.VMEM)],
        out_shape=[struct((2, 4, 4, e, d), BF), struct(clips.shape[1:], BF),
                   struct((4,) + bias.shape, F32)],
        scratch_shapes=[pltpu.VMEM((2, 4, e, d), BF), pltpu.SemaphoreType.DMA((20,)),
                        pltpu.SemaphoreType.DMA((20,)), pltpu.SemaphoreType.DMA((6,))],
        compiler_params=pltpu.CompilerParams(
            collective_id=1, has_side_effects=True, vmem_limit_bytes=LIMIT
        ),
        name="start",
        cost_estimate=cost(50),
    )(qkv, wout, bias, clips)


def weight(w, c):
    v = w[0, c]
    return v.reshape(v.shape[0] * v.shape[1], v.shape[2])


def spatial_body(ids, x, w, gain, shift, qv, bout, *refs):
    stream, n_own, n_send, q, k, v, o, lse, rows = refs[-9:]
    f, r, d = rows.shape
    places = x.shape[-2]

    @pl.when(pl.program_id(0) == 0)
    def _():
        rows[...] = jnp.zeros_like(rows)

    rows[:, :places] = x[...].reshape(f, places, d).astype(F32)
    xv = rows[...].reshape(f * r, d)
    n0 = (hat_of(xv)[0] * gain[0:1] + shift[0:1]).astype(BF)

    def three(m):
        return m.astype(BF).reshape(f, r, d)

    q[...] = three((nt(n0, weight(w, 0)) + qv[0:1]) * HEAD_DIM**-0.5)
    k[...] = three(nt(n0, weight(w, 1)))
    v[...] = three(nt(n0, weight(w, 2)) + qv[1:2])
    for j in range(f):

        def put(at, m, j=j):
            o[j, :, at] = m.astype(BF)

        attend(q.at[j], k.at[j], v.at[j], put, lse.at[j], only_places(places))
    s1 = xv + (nn(o[...].reshape(f * r, d), weight(w, 3)) + bout[0:1])
    stream[...] = s1.reshape(f, r, d)
    n1 = hat_of(s1)[0] * gain[1:2] + shift[1:2]
    parted(n1.reshape(f, r, d), n_own, n_send)


def tokens_spec(near, places, d):
    if near:
        return pl.BlockSpec((1, 2, places, d), lambda i, t: (t[0], i, 0, 0))
    return pl.BlockSpec((2, places, d), lambda i, t: (i, 0, 0))


def spatial(ids, x, w, gain, shift, qv, bout, near, before=()):
    n, places, d = x.shape[-3:]
    steps, frames = n // 2, 2 * n
    begin = 0 if near else steps
    blk = pl.BlockSpec((2, ROWS, d), lambda i, t: (i + begin, 0, 0))
    part = pl.BlockSpec((2, HALF, d), lambda i, t: (i + begin, 0, 0))
    return call(
        spatial_body, "spatial", 12, ids, (steps,),
        [tokens_spec(near, places, d), whole((1,) + w.shape[1:]), whole(gain.shape),
         whole(shift.shape), whole(qv.shape), whole(bout.shape)] + [ANY] * len(before),
        [blk, part, part] + [blk] * 4
        + [pl.BlockSpec((2, d // GROUP, PER * ROWS), lambda i, t: (i + begin, 0, 0))],
        [struct((frames, ROWS, d), F32)] + [struct((frames, HALF, d), BF)] * 2
        + [struct((frames, ROWS, d), BF)] * 4
        + [struct((frames, d // GROUP, PER * ROWS), F32)],
        (x, w, gain, shift, qv, bout) + tuple(before),
        [pltpu.VMEM((2, ROWS, d), F32)],
        {7 + i: i for i in range(len(before))},
    )


def temporal_body(ids, own, got, w, qv, n, q, k, v, o, o_own, o_send, lse):
    i = pl.program_id(0)
    b, r, d = n.shape
    f = own.shape[0]

    @pl.when(i == 0)
    def _():
        in_blocks(own, got, n)
        step = b * r // 4
        ws = [weight(w, c) for c in range(3)]
        for c in range(4):
            at = slice(c * step, (c + 1) * step)
            t = n[...].reshape(b * r, d)[at]
            q[at] = ((nt(t, ws[0]) + qv[2:3]) * HEAD_DIM**-0.5).astype(BF)
            k[at] = nt(t, ws[1]).astype(BF)
            v[at] = (nt(t, ws[2]) + qv[3:4]).astype(BF)

    at = pl.ds(pl.multiple_of(i * r, r), r)

    def put(lanes, m):
        o[0, :, lanes] = m.astype(BF)
        m = m.reshape(2 * f, 1, 8, GROUP)
        o_own[:, :, :, lanes] = m[:f].astype(BF)
        o_send[:, :, :, lanes] = m[f:].astype(BF)

    attend(q.at[at], k.at[at], v.at[at], put, lse.at[0], same_place(place_bias(r)))


def temporal(ids, own, got, w, qv):
    f, half, d = own.shape
    b, r = half // 8, 16 * f
    own, got = own.reshape(f, b, 8, d), got.reshape(f, b, 8, d)
    part = pl.BlockSpec((f, 1, 8, d), lambda i, t: (0, i, 0, 0))
    res = call(
        temporal_body, "temporal", 22, ids, (b,),
        [whole(own.shape), whole(got.shape), whole((1,) + w.shape[1:], (1, 0, 0, 0, 0)),
         whole(qv.shape)],
        [whole((b, r, d))] + [whole((b * r, d))] * 3
        + [pl.BlockSpec((1, r, d), lambda i, t: (i, 0, 0)), part, part,
           pl.BlockSpec((1, d // GROUP, PER * r), lambda i, t: (i, 0, 0))],
        [struct((b, r, d), BF)] + [struct((b * r, d), BF)] * 3 + [struct((b, r, d), BF)]
        + [struct(own.shape, BF)] * 2 + [struct((b, d // GROUP, PER * r), F32)],
        (own, got, w, qv),
    )
    n, q, k, v, o, o_own, o_send, lse = res
    return n, q, k, v, o, o_own.reshape(f, half, d), o_send.reshape(f, half, d), lse


def temporal_back_body(ids, own, got, q, k, v, lse, w, g, dn_own, dn_send, dqkv, do):
    i = pl.program_id(0)
    b, r, d = g.shape
    f = own.shape[0]

    @pl.when(i == 0)
    def _():
        in_blocks(own, got, g)
        wo = weight(w, 3)
        step = b * r // 4
        for c in range(4):
            at = slice(c * step, (c + 1) * step)
            do[at] = nt(g[...].reshape(b * r, d)[at], wo).astype(BF)

    at = pl.ds(pl.multiple_of(i * r, r), r)
    attend_back(
        q, k, v, do.at[at], lse.at[0],
        dqkv.at[0, at], dqkv.at[1, at], dqkv.at[2, at], same_place(place_bias(r)),
    )

    @pl.when(i == pl.num_programs(0) - 1)
    def _():
        ws = [weight(w, c) for c in range(3)]
        acc = nn(dqkv[0], ws[0]) + nn(dqkv[1], ws[1]) + nn(dqkv[2], ws[2])
        for s in range(b):
            m = acc[s * r : (s + 1) * r].reshape(2 * f, 8, d).astype(BF)
            dn_own[:, s] = m[:f]
            dn_send[:, s] = m[f:]


def temporal_back(ids, own, got, q, k, v, lse, w):
    f, half, d = own.shape
    b, r = half // 8, 16 * f
    own, got = own.reshape(f, b, 8, d), got.reshape(f, b, 8, d)
    res = call(
        temporal_back_body, "temporal_back", 34, ids, (b,),
        [whole(own.shape), whole(got.shape)]
        + [pl.BlockSpec((r, d), lambda i, t: (i, 0))] * 3
        + [pl.BlockSpec((1, d // GROUP, PER * r), lambda i, t: (i, 0, 0)),
           whole((1,) + w.shape[1:], (1, 0, 0, 0, 0))],
        [whole((b, r, d)), whole(own.shape), whole(own.shape), whole((3, b * r, d))],
        [struct((b, r, d), BF), struct(own.shape, BF), struct(own.shape, BF),
         struct((3, b * r, d), BF)],
        (own, got, q, k, v, lse, w),
        [pltpu.VMEM((b * r, d), BF)],
    )
    g, dn_own, dn_send, dqkv = res
    return g, dn_own.reshape(f, half, d), dn_send.reshape(f, half, d), dqkv


def weight_grads_body(ids, dqkv, o_in, n, g_in, send, keep, sums, o, g, sem):
    c = pl.program_id(0)

    def loads():
        return [pltpu.make_async_copy(a, b, sem.at[z])
                for z, (a, b) in enumerate(((o_in, o), (g_in, g)))]

    @pl.when(c == 0)
    def _():
        for v in loads():
            v.start()

    d = n.shape[1]
    e = d // 4

    def put(m):
        m = m.astype(BF)
        for r in range(4):
            to = send if r % 2 else keep
            to[r // 2, 0] = m[r * e : (r + 1) * e]

    @pl.when(c < 3)
    def _():
        v = dqkv[0]
        put(tn(v, n[...]))
        sums[0] = jnp.sum(v.astype(F32), axis=0, keepdims=True)

    @pl.when(c == 3)
    def _():
        for v in loads():
            v.wait()
        put(tn(o[...], g[...]))
        sums[0] = jnp.zeros_like(sums[0])


def weight_grads(ids, dqkv, o, n, g):
    d = n.shape[-1]
    rows = n.size // d
    dqkv = dqkv.reshape(3, rows, d)
    o, n, g = (v.reshape(rows, d) for v in (o, n, g))
    out = pl.BlockSpec((2, 1, d // 4, d), lambda c, t: (0, c, 0, 0))
    return call(
        weight_grads_body, "weight_grads", 13, ids, (4,),
        [pl.BlockSpec((1, rows, d), lambda c, t: (jnp.minimum(c, 2), 0, 0))]
        + [ANY, whole((rows, d)), ANY],
        [out, out, pl.BlockSpec((1, 1, d), lambda c, t: (c, 0, 0))],
        [struct((2, 4, d // 4, d), BF)] * 2 + [struct((4, 1, d), F32)],
        (dqkv, o, n, g),
        [pltpu.VMEM((rows, d), BF), pltpu.VMEM((rows, d), BF), pltpu.SemaphoreType.DMA((2,))],
    )


def spatial_back_body(ids, x, s1, dn_own, dn_got, g2, q, k, v, lse, w, gain, shift, *refs):
    g0, sums, dqkv, n0, gb, rows, do = refs[-7:]
    i = pl.program_id(0)
    f, r, d = rows.shape
    places = x.shape[-2]

    @pl.when(i == 0)
    def _():
        sums[...] = jnp.zeros_like(sums)
        rows[...] = jnp.zeros_like(rows)

    def add(at, val):
        sums[at : at + 1] += jnp.sum(val, axis=0, keepdims=True)

    def three(m):
        return m.reshape(f, r, d)

    hat, inv = hat_of(s1[...].reshape(f * r, d))
    dn = joined(dn_own[...], dn_got[...]).reshape(f * r, d)
    add(2, dn * hat)
    add(3, dn)
    g1 = g2[...].reshape(f * r, d) + hat_back(hat, inv, gain[1:2], dn)
    add(4, g1)
    gv = g1.astype(BF)
    gb[...] = three(gv)
    do[...] = three(nt(gv, weight(w, 3)).astype(BF))
    for j in range(f):
        attend_back(
            q.at[j], k.at[j], v.at[j], do.at[j], lse.at[j],
            dqkv.at[0, j], dqkv.at[1, j], dqkv.at[2, j], only_places(places),
        )
    rows[:, :places] = x[...].reshape(f, places, d).astype(F32)
    hat, inv = hat_of(rows[...].reshape(f * r, d))
    n0[...] = three((hat * gain[0:1] + shift[0:1]).astype(BF))
    dn = nn(dqkv[0].reshape(f * r, d), weight(w, 0))
    dn += nn(dqkv[1].reshape(f * r, d), weight(w, 1))
    dn += nn(dqkv[2].reshape(f * r, d), weight(w, 2))
    add(0, dn * hat)
    add(1, dn)
    out = three(g1 + hat_back(hat, inv, gain[0:1], dn))
    g0[...] = out[:, : g0.shape[1]].astype(g0.dtype)


def spatial_back(ids, x, s1, dn_own, dn_got, g2, q, k, v, lse, w, gain, shift, near, before=()):
    frames, _, d = s1.shape
    places = x.shape[-2]
    steps = frames // 4
    begin = 0 if near else steps
    blk = pl.BlockSpec((2, ROWS, d), lambda i, t: (i + begin, 0, 0))
    part = pl.BlockSpec((2, HALF, d), lambda i, t: (i + begin, 0, 0))
    size = places if near else ROWS
    out = pl.BlockSpec((2, size, d), lambda i, t: (i, 0, 0))
    big = struct((frames, ROWS, d), BF)
    return call(
        spatial_back_body, "spatial_back", 20, ids, (steps,),
        [tokens_spec(near, places, d), blk, part, part] + [blk] * 4
        + [pl.BlockSpec((2, d // GROUP, PER * ROWS), lambda i, t: (i + begin, 0, 0)),
           whole((1,) + w.shape[1:]), whole(gain.shape), whole(shift.shape)] + [ANY] * len(before),
        [out, whole((8, d)),
         pl.BlockSpec((3, 2, ROWS, d), lambda i, t: (0, i + begin, 0, 0)), blk, blk],
        [struct((frames // 2, size, d), F32 if near else BF), struct((8, d), F32),
         struct((3, frames, ROWS, d), BF), big, big],
        (x, s1, dn_own, dn_got, g2, q, k, v, lse, w, gain, shift) + tuple(before),
        [pltpu.VMEM((2, ROWS, d), F32), pltpu.VMEM((2, ROWS, d), BF)],
        {13 + i: 2 + i for i in range(len(before))},
    )


def gelu_parts(u):
    cdf = 0.5 + 0.5 * lax.erf(u * 0.7071067811865476)
    return u * cdf, cdf + u * (jnp.exp(-0.5 * u * u) * 0.3989422804014327)


def mlp_load(parts, wt, wd, sem):
    a, b, ct, cd = parts
    x = lax.rem(lax.axis_index("dp"), 2)
    h = a.shape[0] // 2
    mine = pl.ds(pl.multiple_of(x * h, h), h)
    other = pl.ds(pl.multiple_of((1 - x) * h, h), h)
    copies = []
    for z, (w, c) in enumerate(((wt, ct), (wd, cd))):
        rows = pl.ds(z * h, h)
        copies.append(pltpu.make_async_copy(a.at[rows], w.at[0, mine], sem.at[3 * z]))
        copies.append(pltpu.make_async_copy(b.at[rows], w.at[0, other], sem.at[3 * z + 1]))
        copies.append(pltpu.make_async_copy(c, w.at[1], sem.at[3 * z + 2]))
    return copies


def mlp_tile(n2, gb, wt, wd, b, h_s, dr_s):
    u = nt(n2, wt) + b
    dh = nt(gb, wd)
    h, slope = gelu_parts(u)
    h = h.astype(BF)
    h_s[...] = h
    dr = (dh * slope).astype(BF)
    dr_s[...] = dr
    return nn(h, wd), nn(dr, wt)


def mlp_grads(s, n2, gb, h, dr, gwt, gwd, gbi):
    gwt[s] = tn(dr, n2).astype(BF)
    gwd[s] = tn(h, gb).astype(BF)
    gbi[s] = jnp.sum(dr.astype(F32), axis=0, keepdims=True)


def mlp_first_body(ids, s1, o_own, o_got, near, far, w, b, bout, gain, shift, *refs):
    parts = refs[:4]
    (s2, n2, gb, branch, dn, gwt, gwd, gbi,
     n2s, gbs, hs, drs, brs, dns, wt, wd, sem) = refs[4:]
    s, i = pl.program_id(0), pl.program_id(1)
    tile, d = n2.shape
    steps = n2s.shape[0]

    @pl.when((i == 0) & (s == 0))
    def _():
        for c in mlp_load(parts, wt, wd, sem):
            c.start()

    @pl.when(s == 0)
    def _():
        @pl.when(i < steps // 2)
        def _():
            gb[...] = near[...].reshape(tile, d)

        @pl.when(i >= steps // 2)
        def _():
            gb[...] = far[...].reshape(tile, d)

        f, n, _ = o_own.shape

        def flat(v):
            return v[...].astype(F32).reshape(f * n, d).astype(BF)

        wo = w[0, 3]
        turned = jnp.concatenate([wo[r] for r in (1, 0, 3, 2)])
        own = nn(flat(o_own), wo.reshape(d, d)).reshape(f, n, d)
        got = nn(flat(o_got), turned).reshape(f, n, d)
        v = s1[...] + (joined(own, got).reshape(s1.shape) + bout[1:2])
        s2[...] = v
        n = (hat_of(v)[0] * gain[2:3] + shift[2:3]).astype(BF)
        n2[...] = n
        n2s[i] = n
        gbs[i] = gb[...]

    @pl.when((i == 0) & (s == 0))
    def _():
        for c in mlp_load(parts, wt, wd, sem):
            c.wait()

    br, dv = mlp_tile(
        n2s[i], gbs[i], wt[s], wd[s], b[3 - 2 * s, 1:2], hs.at[i], drs.at[i]
    )

    @pl.when(s == 0)
    def _():
        brs[i] = br
        dns[i] = dv

    @pl.when(s == 1)
    def _():
        branch[...] = brs[i] + br
        dn[...] = dns[i] + dv

    @pl.when(i == steps - 1)
    def _():
        rows = steps * tile
        mlp_grads(s, *(v[...].reshape(rows, d) for v in (n2s, gbs, hs, drs)), gwt, gwd, gbi)


def mlp_scratch(steps, tile, d, h):
    return [pltpu.VMEM((steps, tile, d), BF), pltpu.VMEM((steps, tile, d), BF),
            pltpu.VMEM((steps, tile, h), BF), pltpu.VMEM((steps, tile, h), BF),
            pltpu.VMEM((steps, tile, d), F32), pltpu.VMEM((steps, tile, d), F32),
            pltpu.VMEM((2, h, d), BF), pltpu.VMEM((2, h, d), BF), pltpu.SemaphoreType.DMA((6,))]


def mlp_first(ids, s1, o_own, o_got, cot, far, w, b, bout, gain, shift, parts):
    frames, _, d = s1.shape
    tile = 2 * ROWS
    steps = frames // 2
    half = steps // 2
    rows = frames * ROWS
    h = parts[2].shape[0]

    def early(s, i):
        return jnp.where(s == 0, i, steps - 1)

    blk = pl.BlockSpec((tile, d), lambda s, i, t: (early(s, i), 0))
    part = pl.BlockSpec((2, HALF, d), lambda s, i, t: (early(s, i), 0, 0))
    late = pl.BlockSpec((tile, d), lambda s, i, t: (jnp.where(s == 0, 0, i), 0))
    return call(
        mlp_first_body, "mlp_first", 33, ids, (2, steps),
        [blk, part, part,
         pl.BlockSpec((2, ROWS, d), lambda s, i, t: (jnp.minimum(early(s, i), half - 1), 0, 0)),
         pl.BlockSpec((2, ROWS, d), lambda s, i, t: (jnp.maximum(early(s, i) - half, 0), 0, 0)),
         whole((1, 4) + w.shape[2:], (1, 0, 0, 0, 0)), whole(b.shape), whole(bout.shape),
         whole(gain.shape), whole(shift.shape)] + [ANY] * 4,
        [blk] * 3 + [late] * 2 + [whole((2, h, d)), whole((2, h, d)), whole((2, 1, h))],
        [struct((rows, d), F32), struct((rows, d), BF), struct((rows, d), BF),
         struct((rows, d), F32), struct((rows, d), F32), struct((2, h, d), BF),
         struct((2, h, d), BF), struct((2, 1, h), F32)],
        (s1.reshape(rows, d), o_own, o_got, cot, far, w, b, bout, gain, shift) + tuple(parts),
        mlp_scratch(steps, tile, d, h),
    )


def mlp_second_body(ids, s2, n2, gb, br0, dn0, b, bdown, gain, *refs):
    parts = refs[:4]
    (near, far, g2, g_own, g_send, gwt, gwd, gbi, sums,
     n2s, gbs, hs, drs, brs, dns, wt, wd, sem) = refs[4:]
    s, i = pl.program_id(0), pl.program_id(1)
    tile, d = n2.shape
    steps = n2s.shape[0]

    @pl.when((i == 0) & (s == 0))
    def _():
        sums[...] = jnp.zeros_like(sums)
        for c in mlp_load(parts, wt, wd, sem):
            c.start()

    @pl.when(s == 0)
    def _():
        n2s[i] = n2[...]
        gbs[i] = gb[...]

    @pl.when((i == 0) & (s == 0))
    def _():
        for c in mlp_load(parts, wt, wd, sem):
            c.wait()

    br, dv = mlp_tile(
        n2s[i], gbs[i], wt[s], wd[s], b[2 - 2 * s, 1:2], hs.at[i], drs.at[i]
    )

    @pl.when(s == 0)
    def _():
        brs[i] = br0[...] + br
        dns[i] = dn0[...] + dv

    @pl.when(i == steps - 1)
    def _():
        rows = steps * tile
        mlp_grads(s, *(v[...].reshape(rows, d) for v in (n2s, gbs, hs, drs)), gwt, gwd, gbi)

    @pl.when(s == 1)
    def _():
        def add(at, val):
            sums[at : at + 1] += jnp.sum(val, axis=0, keepdims=True)

        v = s2[...]
        f, places, _ = near.shape
        out = (v + (brs[i] + br + bdown[...])).reshape(f, ROWS, d)

        @pl.when(i < steps // 2)
        def _():
            near[...] = out[:, :places]

        @pl.when(i >= steps // 2)
        def _():
            far[...] = out.astype(BF)

        hat, inv = hat_of(v)
        dt = dns[i] + dv
        add(0, dt * hat)
        add(1, dt)
        g3 = gbs[i].astype(F32)
        add(3, g3)
        g = g3 + hat_back(hat, inv, gain[2:3], dt)
        add(2, g)
        g = g.reshape(f, ROWS, d)
        g2[...] = g
        parted(g, g_own, g_send)


def mlp_second(ids, s2, n2, gb, br0, dn0, b, bdown, gain, parts, shape):
    rows, d = s2.shape
    _, n, places, _ = shape
    frames = rows // ROWS
    steps = frames // 2
    half = steps // 2
    tile = 2 * ROWS
    h = parts[2].shape[0]

    def late(s, i):
        return jnp.where(s == 0, 0, i)

    blk = pl.BlockSpec((tile, d), lambda s, i, t: (jnp.where(s == 0, i, steps - 1), 0))
    end = pl.BlockSpec((tile, d), lambda s, i, t: (late(s, i), 0))
    three = pl.BlockSpec((2, ROWS, d), lambda s, i, t: (late(s, i), 0, 0))
    part = pl.BlockSpec((2, HALF, d), lambda s, i, t: (late(s, i), 0, 0))
    return call(
        mlp_second_body, "mlp_second", 33, ids, (2, steps),
        [end] + [blk] * 4 + [whole(b.shape), whole(bdown.shape), whole(gain.shape)] + [ANY] * 4,
        [pl.BlockSpec((2, places, d), lambda s, i, t: (jnp.minimum(late(s, i), half - 1), 0, 0)),
         pl.BlockSpec((2, ROWS, d), lambda s, i, t: (jnp.maximum(late(s, i) - half, 0), 0, 0)),
         three, part, part, whole((2, h, d)), whole((2, h, d)), whole((2, 1, h)), whole((8, d))],
        [struct((n, places, d), F32), struct((n, ROWS, d), BF), struct((frames, ROWS, d), F32),
         struct((frames, HALF, d), BF), struct((frames, HALF, d), BF), struct((2, h, d), BF),
         struct((2, h, d), BF), struct((2, 1, h), F32), struct((8, d), F32)],
        (s2, n2, gb, br0, dn0, b, bdown, gain) + tuple(parts),
        mlp_scratch(steps, tile, d, h),
    )


def both_clips_body(ids, near, got, out):
    mine = pl.program_id(0) == ids[0]
    f, places, _ = near.shape

    @pl.when(mine)
    def _():
        for j in range(f):
            out[0, :, j] = near[j]

    @pl.when(jnp.logical_not(mine))
    def _():
        for j in range(f):
            out[0, :, j] = got[j, :places].astype(F32)


def both_clips(ids, near, got):
    n, places, d = near.shape
    out = call(
        both_clips_body, "both_clips", 6, ids, (2,),
        [whole(near.shape), whole(got.shape)],
        pl.BlockSpec((1, places, n, d), lambda i, t: (i, 0, 0, 0)),
        struct((2, places, n, d), F32),
        (near, got),
    )
    return out.transpose(0, 2, 1, 3)


def shape_body(ids, f0, f1, m, mo, gqkv, gout, gwin, gwd):
    x = lax.rem(lax.axis_index("dp"), 2)
    for i, f in enumerate((f0, f1)):
        for c in range(3):
            gqkv[i, c] = f[c].astype(F32)
        gout[i] = f[3].astype(F32)
    n = m.shape[0] // 2
    lo = jnp.where(x == 0, m[...], mo[...]).astype(F32)
    hi = jnp.where(x == 0, mo[...], m[...]).astype(F32)
    gwin[:, :n] = lo[:n].T
    gwin[:, n:] = hi[:n].T
    gwd[:n] = lo[n:]
    gwd[n:] = hi[n:]


def to_results(ids, f0, f1, m, mo):
    _, e, d = f0.shape
    h = m.shape[0]
    shapes = [(2, 3, e, d), (2, e, d), (d, h), (h, d)]
    return call(
        shape_body, "to_results", 5, ids, (1,),
        [whole(v.shape) for v in (f0, f1, m, mo)],
        [whole(v) for v in shapes],
        [struct(v, F32) for v in shapes],
        (f0, f1, m, mo),
    )


def finish_body(dp, t0, t1, rel, rep, f0, f1, rel_o, rep_o, *scratch):
    (tt, zr, ta, tb, aa, ab, xs, rel_r, rep_r, rel_s, rep_s, send, recv) = scratch
    me_d, me_t = lax.axis_index("dp"), lax.axis_index("tensor")
    x = lax.rem(me_d, 2)
    bits = []
    bit = 2
    while bit < dp:
        bits.append(bit)
        bit *= 2

    def flip(v, b):
        return v + b - 2 * b * lax.rem(v // b, 2)

    def core():
        return (me_d, flip(me_t, 1))

    def over_y():
        return (me_d, flip(me_t, 2))

    def over_d(b):
        return (flip(me_d, b), me_t)

    partners = [core(), over_y(), over_d(1)] + [over_d(b) for b in bits]
    barrier = pltpu.get_barrier_semaphore()
    for p in partners:
        pl.semaphore_signal(barrier, inc=1, device_id=p, device_id_type=pl.DeviceIdType.MESH)
    pl.semaphore_wait(barrier, len(partners))

    count = [0]

    def copy(src, dst, to):
        k = count[0]
        count[0] += 1
        c = pltpu.make_async_remote_copy(
            src_ref=src, dst_ref=dst, send_sem=send.at[k], recv_sem=recv.at[k],
            device_id=to, device_id_type=pl.DeviceIdType.MESH,
        )
        c.start()
        return c

    def plus(a, b):
        return (a.astype(F32) + b.astype(F32)).astype(BF)

    n = tt.shape[1]

    def rest(k, out):
        size, held = n, tt.at[k]
        done = []
        for z, b in enumerate(bits[:2]):
            half = size // 2
            bitv = lax.rem(me_d // b, 2)
            mine = pl.multiple_of(bitv * half, 16)
            other = pl.multiple_of((1 - bitv) * half, 16)
            dst = zr.at[k, z, pl.ds(0, half)]
            c = copy(held.at[pl.ds(other, half)], dst, over_d(b))
            yield
            c.wait()
            nxt = (ta if z == 0 else tb).at[k]
            nxt[...] = plus(held[pl.ds(mine, half)], dst[...])
            done.append(((aa if z == 0 else ab).at[k], mine, half, b))
            size, held = half, nxt
        for z, b in enumerate(bits[2:]):
            dst = zr.at[k, 2 + z, pl.ds(0, size)]
            c = copy(held, dst, over_d(b))
            yield
            c.wait()
            held[...] = plus(held[...], dst[...])
        for z, (up, mine, half, b) in enumerate(reversed(done)):
            up[pl.ds(mine, half)] = held[...]
            c = copy(up.at[pl.ds(mine, half)], up.at[pl.ds(mine, half)], over_d(b))
            yield
            c.wait()
            held = up
        c = copy(held, xs.at[k, 0], over_d(1))
        yield
        c.wait()
        out(held, xs.at[k, 0])

    def attn0(j):
        tt[j] = t0[j]

        def out(mine, got):
            f0[j + 2 * x] = mine[...]
            f0[j + 2 * (1 - x)] = got[...]

        yield from rest(j, out)

    def attn1():
        c = copy(t1, xs.at[2], over_d(1))
        f1[pl.ds(2 * x, 2)] = t1[...]
        yield
        yield
        yield
        c.wait()
        f1[pl.ds(2 - 2 * x, 2)] = xs[2]

    def small():
        rel_s[...] = rel[...]
        rep_s[...] = rep[...]
        for z, (to, b) in enumerate([(core(), 1), (over_y(), 2)]):
            c = [copy(rel_s, rel_r.at[z], to), copy(rep_s, rep_r.at[z], to)]
            yield
            for v in c:
                v.wait()
            rep_s[...] += rep_r[z]
            for r in range(4):
                rel_s[r] = rel_s[r] + rel_r[z, r ^ b]
        for z, b in enumerate([1] + bits):
            c = [
                copy(rel_s.at[0], rel_r.at[2 + z, 0], over_d(b)),
                copy(rep_s, rep_r.at[2 + z], over_d(b)),
            ]
            yield
            for v in c:
                v.wait()
            rep_s[...] += rep_r[2 + z]
            rel_s[0] = rel_s[0] + rel_r[2 + z, 0]
        rel_o[...] = rel_s[0]
        rep_o[...] = rep_s[...]

    chains = [attn0(0), attn0(1), attn1(), small()]
    while chains:
        left = []
        for chain in chains:
            try:
                next(chain)
                left.append(chain)
            except StopIteration:
                pass
        chains = left


def finish(t0, t1, rel, rep, dp):
    _, n, d = t0.shape
    nb = max(dp.bit_length() - 2, 0)
    vm = pl.BlockSpec(memory_space=pltpu.VMEM)
    return pl.pallas_call(
        functools.partial(finish_body, dp),
        in_specs=[vm] * 4,
        out_specs=[vm] * 4,
        out_shape=[struct((4, n, d), BF)] * 2 + [struct(rel.shape[1:], F32), struct(rep.shape, F32)],
        scratch_shapes=[
            pltpu.VMEM((2, n, d), BF),
            pltpu.VMEM((2, max(nb, 1), n // 2, d), BF),
            pltpu.VMEM((2, n // 2, d), BF),
            pltpu.VMEM((2, n // 4, d), BF),
            pltpu.VMEM((2, n, d), BF),
            pltpu.VMEM((2, n // 2, d), BF),
            pltpu.VMEM((3, 2, n, d), BF),
            pltpu.VMEM((3 + nb,) + rel.shape, F32),
            pltpu.VMEM((3 + nb,) + rep.shape, F32),
            pltpu.VMEM(rel.shape, F32),
            pltpu.VMEM(rep.shape, F32),
            pltpu.SemaphoreType.DMA((96,)),
            pltpu.SemaphoreType.DMA((96,)),
        ],
        compiler_params=pltpu.CompilerParams(
            collective_id=0, has_side_effects=True, vmem_limit_bytes=LIMIT
        ),
        name="finish",
        cost_estimate=cost(40),
    )(t0, t1, rel, rep)


def shards(clips, cot, gain, shift, qkv, qvb, wout, bout, win, b_in, wdown, bdown):
    tensor = lax.axis_index("tensor")
    y = tensor // 2
    x = lax.axis_index("dp") % 2
    dp = lax.axis_size("dp")
    width = clips.shape[-1]
    e = qkv.shape[-1]
    h = win.shape[1] // 2
    ids = y.reshape(1).astype(jnp.int32)

    def over_tensor(v, bit):
        return lax.ppermute(v, "tensor", [(i, i ^ bit) for i in range(4)])

    def over_dp(v, bit):
        return lax.ppermute(v, "dp", [(i, i ^ bit) for i in range(dp)])

    def after(v, *others):
        return lax.optimization_barrier((v,) + others)[0]

    def pick(v, axis):
        n = v.shape[axis] // 2
        return (
            lax.dynamic_slice_in_dim(v, x * n, n, axis),
            lax.dynamic_slice_in_dim(v, (1 - x) * n, n, axis),
        )

    def padded(v):
        return jnp.pad(v, ((0, 0), (0, ROWS - v.shape[1]), (0, 0)))

    bias = jnp.concatenate([qvb.reshape(1, -1), b_in.reshape(1, -1), jnp.zeros((6, width), F32)])
    w, clips_far, b = start(qkv.transpose(0, 1, 3, 2), wout, bias, clips)
    win_t = win.T
    z = lax.axis_index("dp") // 2 % 2
    n = h // 2
    at = x * h + z * n
    sent = [jnp.concatenate([lax.dynamic_slice_in_dim(v, at, n, 0) for v in (win_t, wdown)])]
    sent.append(padded(lax.dynamic_index_in_dim(cot, 1 - y, 0, False)))
    w, *sent = lax.optimization_barrier((w, *sent))
    m_q = over_tensor(sent[0], 2)
    cot_far = over_tensor(sent[1], 2)
    m_c = [over_tensor(after(v, w), 1) for v in (win_t, wdown)]
    qv = b[:, 0].reshape(4, 4, e).transpose(1, 0, 2).reshape(4, width)

    some = spatial(ids, clips, w, gain, shift, qv, bout, True)
    clips_far, m_q = lax.optimization_barrier((clips_far, m_q))
    m_z = over_dp(m_q, 2)
    s1, n_own, n_send, q0, k0, v0, o0, lse0 = spatial(
        ids, clips_far, w, gain, shift, qv, bout, False, some
    )
    n_own, m_z = lax.optimization_barrier((n_own, m_z))
    m_a, m_b = jnp.where(z == 0, m_q, m_z), jnp.where(z == 0, m_z, m_q)
    m_y = jnp.concatenate([m_a[:n], m_b[:n], m_a[n:], m_b[n:]])
    m_x = over_dp(m_y, 1)
    m_cy = over_tensor(m_y, 1)
    n1p, q1, k1, v1, o1p, o_own, o_send, lse1 = temporal(
        ids, n_own, over_tensor(n_send, 1), w, qv
    )
    m_cx = over_tensor(m_x, 1)
    cot_near = padded(lax.dynamic_index_in_dim(after(cot, w), y, 0, False))

    first = (m_cy, m_cx, m_c[0], m_c[1])
    second = (m_y, m_x, win_t, wdown)
    s2, n2, gb3, branch, dn2, gwt_a, gwd_a, gb_a = mlp_first(
        ids, s1, o_own, over_tensor(o_send, 1), cot_near, cot_far, w, b, bout, gain, shift, first
    )
    out_near, far, g2, g_own, g_send, gwt_b, gwd_b, gb_b, sums2 = mlp_second(
        ids, s2, n2, gb3, branch, dn2, b, bdown[None], gain, second, clips.shape
    )

    g_got = over_tensor(g_send, 1)
    keep_t = gwt_b + over_tensor(gwt_a, 1)
    keep_d = gwd_b + over_tensor(gwd_a, 1)
    g_got, keep_t, keep_d = lax.optimization_barrier((g_got, keep_t, keep_d))
    got_t = over_tensor(keep_t[0], 2)
    mine_d, send_d = pick(keep_d, 1)
    got_d = over_dp(send_d, 1)
    out_got = over_tensor(after(far, got_t), 2)

    g2p, dn_own, dn_send, dqkv1 = temporal_back(ids, g_own, g_got, q1, k1, v1, lse1, w)
    dn_got = over_tensor(dn_send, 1)
    mine_t, send_t = pick(keep_t[1] + got_t, 0)
    mine_d = mine_d + got_d
    g2p, mine_t, send_t, mine_d = lax.optimization_barrier((g2p, mine_t, send_t, mine_d))
    got_t = over_dp(send_t, 1)
    got_d = over_tensor(mine_d[0], 2)
    gs1, gk1, sums1 = weight_grads(ids, dqkv1, o1p, n1p, g2p)
    mlp_sum = jnp.concatenate([mine_t + got_t, mine_d[1] + got_d])
    dn_got, gs1, mlp_sum = lax.optimization_barrier((dn_got, gs1, mlp_sum))
    groups = [[i for i in range(dp) if i % 2 == p] for p in range(2)]
    if dp > 2:
        mlp_sum = lax.psum(mlp_sum, "dp", axis_index_groups=groups)
    got1 = over_tensor(gs1, 1)
    kept = (s1, dn_own, dn_got, g2, q0, k0, v0, lse0, w, gain, shift)
    g0_far, sums_f, *rest = spatial_back(ids, clips_far, *kept, False)
    mine1, send1 = pick(gk1 + got1, 1)
    rest[0], mine1, send1, out_got = lax.optimization_barrier((rest[0], mine1, send1, out_got))
    got_x = over_dp(send1[0], 1)
    got_y = over_tensor(mine1[1], 2)
    got_xy = lax.ppermute(
        send1[1], ("dp", "tensor"), [(i, ((i // 4) ^ 1) * 4 + (i % 4 ^ 2)) for i in range(4 * dp)]
    )
    grad_near, sums_n, dqkv0, n0, gb0 = spatial_back(ids, clips, *kept, True, rest)
    t1 = (mine1[0] + got_x) + (got_y + got_xy)
    gb0, t1, mlp_sum = lax.optimization_barrier((gb0, t1, mlp_sum))
    gs0, gk0, sums_b = weight_grads(ids, dqkv0, o0, n0, gb0)

    bits = [1 << k for k in range(1, dp.bit_length() - 1)]
    z1 = over_dp(t1, bits[0]) if bits else jnp.zeros_like(t1)
    gs0, gk0, z1 = lax.optimization_barrier((gs0, gk0, z1))
    t1 = t1 + z1
    ta, tb = t1[0], t1[1]
    for bit in bits[1:]:
        ta = ta + over_dp(ta, bit)
    got0 = over_tensor(gs0, 1)
    output = both_clips(ids, out_near, after(out_got, gs0))
    keep0 = (gk0 + got0).reshape(2, 2, 2, e, width)
    mine0, send0 = (v[:, 0] for v in pick(keep0, 1))
    got_y = over_tensor(jnp.stack([mine0[1, 0], send0[1, 0]]), 2)
    got_x = over_dp(send0[:, 1], 1)
    mlp_got = over_dp(mlp_sum, 1)
    output, got_y, got_x, ta, tb = lax.optimization_barrier((output, got_y, got_x, ta, tb))
    for bit in bits[1:]:
        tb = tb + over_dp(tb, bit)
    in_got = over_tensor(after(g0_far, got_y), 2)
    got_a = over_dp(send0[0, 0] + got_y[1], 1)
    got_b = over_tensor(mine0[1, 1] + got_x[1], 2)
    got_a, got_b, tb = lax.optimization_barrier((got_a, got_b, tb))
    t1 = jnp.stack([ta, tb])
    t0 = jnp.stack([mine0[0, 0] + got_y[0] + got_a, mine0[0, 1] + got_x[0] + got_b])
    sums0 = sums_f + sums_n
    rep = jnp.stack(
        [sums0[0], sums0[2], sums2[0], sums0[1], sums0[3], sums2[1], sums0[4], sums2[2], sums2[3]]
    )
    rep = jnp.pad(rep, ((0, 7), (0, 0)))
    qvs = jnp.stack([sums_b[0, 0], sums_b[2, 0], sums1[0, 0], sums1[2, 0]])
    qvs = qvs.reshape(4, 4, e).transpose(1, 0, 2).reshape(4, 1, 4 * e)
    hid = jnp.stack([gb_b[1], gb_a[1], gb_b[0], gb_a[0]])
    rel = jnp.concatenate([qvs, hid, jnp.zeros((4, 6, width), F32)], axis=1)
    f0, f1, rel, rep = finish(t0, t1, rel, rep, dp)
    input_grad = both_clips(ids, grad_near, after(in_got, f0))
    gqkv, gout, gwin, gwd = to_results(ids, f0, f1, mlp_sum, mlp_got)
    gqkv = gqkv.transpose(0, 1, 3, 2)
    return (
        output,
        input_grad,
        rep[0:3],
        rep[3:6],
        gqkv,
        rel[0].reshape(2, 2, e),
        gout,
        rep[6:8],
        gwin,
        rel[1],
        gwd,
        rep[8],
    )


def solution(mesh):
    placed = (
        P("dp", "tensor", None, None),
        P("dp", "tensor", None, None),
        P(),
        P(),
        P(None, None, None, "tensor"),
        P(None, None, "tensor"),
        P(None, "tensor", None),
        P(),
        P(None, "tensor"),
        P("tensor"),
        P("tensor", None),
        P(),
    )
    return jax.shard_map(
        shards,
        mesh=mesh,
        in_specs=placed,
        out_specs=(
            P("dp", "tensor", None, None),
            P("dp", "tensor", None, None),
            P(),
            P(),
            P(None, None, None, "tensor"),
            P(None, None, "tensor"),
            P(None, "tensor", None),
            P(),
            P(None, "tensor"),
            P("tensor"),
            P("tensor", None),
            P(),
        ),
        check_vma=False,
    )
```
